128 devices in a mesh: section: 4 (over z), dp: 32 (over y, x, core).
Axes of the slice: x: 4, y: 4, z: 4, core: 2. Of those that a mesh axis runs over, the one named last changes fastest.
Arguments:
- saved: bfloat16 [4, 128, 4, 8, 384], P('section', 'dp'), may hold values from -6 to 6
- kernels: bfloat16 [4, 384, 3, 3, 384], P('section'), may hold values from -0.109375 to 0.109375
- head: bfloat16 [384, 512], replicated, may hold values from -0.3125 to 0.3125
- counts: int32 [32], P('dp'), may hold values from 1 to 4, as said below
- pairs: int32 [128], P('dp'), may hold values from 0 to 127, as said below
- valid: int32 [128], P('dp'), may hold values 0 or 1
Outputs:
- input_grads: bfloat16 [4, 128, 4, 8, 384], P('section', 'dp')
- weight_grads: float32 [4, 384, 3, 3, 384], P('section', 'dp')
- head_grad: float32 [384, 512], P('dp', 'section')
The draws below stay inside these ranges and needn't reach their ends.
Inputs may be any that keep to these rules, and one draw needn't show every extreme that they name: Slot d * 4 + r holds a record exactly when r < counts[d]; at least one index of dp holds 4 records. pairs[pairs[i]] = i and pairs[i] != i.
All inputs are finite; a program needn't handle non-finite values. No bound on the sum of `valid` on one device may be relied on, other than what follows from the above.
Results may differ from the reference program's by a relative error of at most 0.012.
Values may be sent and summed in bfloat16 or wider, within the bound.
No kernel may reach another device: no remote copies, remote signals or barrier semaphores. Data moves between devices by JAX's collectives and lax.ppermute only.
A program may use at most 64 MiB of HBM per device.

```python
import jax
import jax.numpy as jnp
from jax import lax

CH = 384
EMB = 512
KS = 3
PH = 4
PW = 8
CAP = 4
RECS = 128
N_SECTION = 4


def draw_counts(key, part):
    groups = RECS // CAP
    lowest = max(1, CAP // 4)
    first_key, second_key = jax.random.split(key)
    values = jax.random.randint(first_key, (groups,), lowest, CAP + 1)
    fullest = jax.random.randint(second_key, (), 0, groups)
    return jnp.where(jnp.arange(groups) == fullest, CAP, values).astype(jnp.int32)


def draw_pairs(key, part):
    order = jax.random.permutation(key, RECS).astype(jnp.int32)
    mates = order.reshape(RECS // 2, 2)[:, ::-1].reshape(RECS)
    return jnp.zeros((RECS,), jnp.int32).at[order].set(mates)


def place_ends(values, stream_key, smallest, top_value):
    dims = values.shape
    index_at = [jax.random.randint(jax.random.fold_in(stream_key, axis), (), 0, dims[axis]) for axis in range(len(dims))]
    values = values.at[tuple(index_at)].set(smallest)
    longest = dims.index(max(dims))
    index_at[longest] = (index_at[longest] + 1) % dims[longest]
    return values.at[tuple(index_at)].set(top_value)


def level_of(rng, shape, cuts, low, high):
    def one(dim, parts):
        steps = jax.random.uniform(jax.random.fold_in(jax.random.fold_in(rng, 6), dim), (parts,), jnp.float32, low / len(cuts), high / len(cuts))
        return jnp.repeat(jnp.exp(steps), shape[dim] // parts).reshape((-1,) + (1,) * (len(shape) - dim - 1))

    gain = one(*cuts[0])
    for cut in cuts[1:]:
        gain = gain * one(*cut)
    return gain


def scatter_about(rng, extent, deviation, reach, shards=(), kind=jnp.bfloat16):
    result = deviation * jax.random.normal(rng, extent, jnp.float32)
    if shards:
        result = result * level_of(rng, extent, shards, -0.22, 0.18)
    return jnp.clip(result, -reach, reach).astype(kind)


def setup_inputs(seed: int = 0) -> dict:
    arg_keys = jax.random.split(jax.random.key(seed), 7)
    saved = scatter_about(arg_keys[0], (N_SECTION, RECS, PH, PW, CH), 1.0, 6.0, ((0, 4), (1, 32)))
    kernels = scatter_about(arg_keys[1], (N_SECTION, CH, KS, KS, CH), (KS * KS * CH) ** -0.5, 0.109375, ((0, 4),))
    head = scatter_about(arg_keys[2], (CH, EMB), CH ** -0.5, 0.3125)
    counts = draw_counts(jax.random.fold_in(arg_keys[6], 71), 0)
    pairs = draw_pairs(jax.random.fold_in(arg_keys[6], 71), 0)
    valid = place_ends((jax.random.randint(arg_keys[5], (RECS,), 0, 8) < 7).astype(jnp.int32), jax.random.fold_in(arg_keys[5], 1), 0, 1)
    return dict(saved=saved, kernels=kernels, head=head, counts=counts, pairs=pairs, valid=valid)


tau_value = 0.2
loss_scale = 32.0
norm_eps = 1e-06

def conv_apply(inputs, kernel):
    return lax.conv_general_dilated(inputs, kernel, (1, 1), 'SAME', dimension_numbers=('NHWC', 'IHWO', 'NHWC'), preferred_element_type=jnp.float32)

def conv_back(grads, kernel):
    return lax.conv_general_dilated(grads, jnp.flip(kernel, (1, 2)), (1, 1), 'SAME', dimension_numbers=('NHWC', 'OHWI', 'NHWC'), preferred_element_type=jnp.float32)

def kernel_grad(inputs, grads):
    return lax.conv_general_dilated(inputs, grads, (1, 1), ((1, 1), (1, 1)), dimension_numbers=('CHWN', 'IHWO', 'NHWC'), preferred_element_type=jnp.float32)

def reference(saved, kernels, head, counts, pairs, valid):
    slot = jnp.arange(RECS, dtype=jnp.int32)
    owner = slot // CAP
    live = jnp.where((slot - owner * CAP < counts[owner]) & (valid == 1), 1.0, 0.0).astype(jnp.float32)
    slopes = []
    pooled = None
    for layer in range(N_SECTION):
        pre = conv_apply(saved[layer], kernels[layer])
        sigma = jax.nn.sigmoid(pre)
        slopes.append(sigma * (1.0 + pre * (1.0 - sigma)))
        if layer == N_SECTION - 1:
            pooled = lax.optimization_barrier(jnp.mean(saved[layer].astype(jnp.float32) + pre * sigma, axis=(1, 2))).astype(jnp.bfloat16)
    proj = jnp.dot(pooled, head, preferred_element_type=jnp.float32)
    inv = lax.rsqrt(lax.optimization_barrier(jnp.sum(proj * proj, axis=1, keepdims=True)) + norm_eps)
    unit = proj * inv
    unit_b = unit.astype(jnp.bfloat16)
    scores = lax.dot_general(unit_b, unit_b, (((1,), (1,)), ((), ())), preferred_element_type=jnp.float32) / tau_value
    expo = jnp.where(slot[:, None] != slot[None, :], jnp.exp(scores), 0.0)
    total = lax.optimization_barrier(jnp.sum(expo * live[None, :], axis=1))
    share = live * live[pairs]
    coef = lax.optimization_barrier((share / total).astype(jnp.bfloat16)).astype(jnp.float32)
    mixing = expo * (coef[:, None] * live[None, :] + coef[None, :] * live[:, None]) - 2.0 * jnp.where(pairs[:, None] == slot[None, :], share[:, None], 0.0)
    dunit = jnp.dot(mixing.astype(jnp.bfloat16), unit_b, preferred_element_type=jnp.float32) * (loss_scale / tau_value)
    along = lax.optimization_barrier(jnp.sum(unit * dunit, axis=1, keepdims=True))
    dproj = ((dunit - unit * along) * inv).astype(jnp.bfloat16)
    head_grad = lax.dot_general(pooled, dproj, (((0,), (0,)), ((), ())), preferred_element_type=jnp.float32)
    dpooled = lax.dot_general(dproj, head, (((1,), (1,)), ((), ())), preferred_element_type=jnp.float32).astype(jnp.bfloat16)
    top = (dpooled.astype(jnp.float32) / (PH * PW)).astype(jnp.bfloat16)
    cotan = jnp.broadcast_to(top[:, None, None, :], (RECS, PH, PW, CH))
    grads_in = []
    grads_w = []
    for layer in range(N_SECTION - 1, -1, -1):
        dpre = (cotan.astype(jnp.float32) * slopes[layer]).astype(jnp.bfloat16)
        cotan = (cotan.astype(jnp.float32) + conv_back(dpre, kernels[layer])).astype(jnp.bfloat16)
        grads_in.insert(0, cotan)
        grads_w.insert(0, kernel_grad(saved[layer], dpre))
    return (jnp.stack(grads_in), jnp.stack(grads_w), head_grad)
```

```python
import functools

import jax
import jax.numpy as jnp
from jax import lax
from jax.experimental import pallas as pl
from jax.experimental.pallas import tpu as pltpu
from jax.sharding import PartitionSpec as P

tau_value = 0.2
loss_scale = 32.0
norm_eps = 1e-06
VMEM = pltpu.VMEM
SMEM = pltpu.SMEM
ANY = pl.ANY
f32 = jnp.float32
bf16 = jnp.bfloat16
NN = (((1,), (0,)), ((), ()))
NT = (((1,), (1,)), ((), ()))

ROWS, CELLS, CH, EMB = 128, 32, 384, 512
MSG = 144


def mm(a, b, dims=NN):
    return lax.dot_general(a, b, dims, preferred_element_type=f32)


def row_iota(shape):
    return lax.broadcasted_iota(jnp.int32, shape, 0)


def col_iota(shape):
    return lax.broadcasted_iota(jnp.int32, shape, 1)


def position():
    rank = lax.axis_index("dp")
    return lax.axis_index("section"), rank, (rank >> 3), ((rank >> 1) & 3), (rank & 1)


def column_shifts(v):
    pw = row_iota((ROWS, 1)) & 7
    left = jnp.where(pw > 0, pltpu.roll(v, 1, 0), 0.0)
    right = jnp.where(pw < 7, pltpu.roll(v, ROWS - 1, 0), 0.0)
    return left, v, right


def row_shift(v, dh):
    if dh == 0:
        return v
    v = v.reshape(4, CELLS, CH)
    zero = jnp.zeros((4, 8, CH), v.dtype)
    if dh > 0:
        v = jnp.concatenate([v[:, 8:], zero], axis=1)
    else:
        v = jnp.concatenate([zero, v[:, :24]], axis=1)
    return v.reshape(ROWS, CH)


def weight_copies(w_hbm, w, sem):
    return [pltpu.make_async_copy(w_hbm.at[kh], w.at[kh], sem.at[kh]) for kh in range(3)]


def conv_back(dpre, w, copies):
    cols = column_shifts(dpre)
    total = None
    for kh in range(3):
        lhs = jnp.concatenate(
            [row_shift(cols[2 - kw], 1 - kh).astype(bf16) for kw in range(3)], axis=1
        )
        copies[kh].wait()
        rhs = jnp.concatenate([w[kh, kw] for kw in range(3)], axis=1)
        part = mm(lhs, rhs, NT)
        total = part if total is None else total + part
    return total


def forward_kernel(saved, w_hbm, counts, pairs, valid, slope, message, w, sem):
    copies = weight_copies(w_hbm, w, sem)
    for copy in copies:
        copy.start()
    v = saved[...].astype(f32)
    cols = column_shifts(v)
    pre = None
    for kh in range(3):
        lhs = jnp.concatenate(
            [row_shift(cols[kw], kh - 1).astype(bf16) for kw in range(3)], axis=1
        )
        copies[kh].wait()
        part = mm(lhs, w[kh].reshape(3 * CH, CH))
        pre = part if pre is None else pre + part
    sigma = jax.nn.sigmoid(pre)
    slope[...] = sigma * (1.0 + pre * (1.0 - sigma))
    feature = (v + pre * sigma).reshape(4, CELLS, CH)
    pooled = jnp.sum(feature, axis=1) / CELLS
    at = (row_iota((4, 128)), col_iota((4, 128)))
    extra = jnp.zeros((4, 128), f32)
    for slot in range(4):
        alive = jnp.logical_and(slot < counts[0], valid[slot] == 1)
        here = at[0] == slot
        extra = jnp.where(
            jnp.logical_and(here, at[1] == 0), jnp.where(alive, 1.0, 0.0).astype(f32), extra
        )
        extra = jnp.where(
            jnp.logical_and(here, at[1] == 1), pairs[slot].astype(f32), extra
        )
    packed = jnp.concatenate(
        [pooled[:, :256], jnp.concatenate([pooled[:, 256:], extra], axis=1)], axis=0
    )
    pair = jnp.concatenate([packed, packed], axis=0).astype(bf16)
    for at_row in range(0, 256, 16):
        message[at_row : at_row + 16, :] = pair


def contrast(gathered, head, rank):
    slot = row_iota((128, 256))
    lane = col_iota((128, 256))
    home = ((slot >> 2) << 3) + (slot & 3)
    first = mm(jnp.where(lane == home, 1.0, 0.0).astype(bf16), gathered)
    second = mm(jnp.where(lane == home + 4, 1.0, 0.0).astype(bf16), gathered)
    pooled = jnp.concatenate([first, second[:, :128]], axis=1).astype(bf16)
    live = second[:, 128:129]
    pairs = second[:, 129:130]
    proj = mm(pooled, head)
    inv = lax.rsqrt(jnp.sum(proj * proj, axis=1, keepdims=True) + norm_eps)
    unit = proj * inv
    unit_b = unit.astype(bf16)
    i = row_iota((128, 128))
    j = col_iota((128, 128))
    same = i == j

    def across(column):
        return jnp.sum(jnp.where(same, column, 0.0), axis=0, keepdims=True)

    expo = jnp.where(same, 0.0, jnp.exp(mm(unit_b, unit_b, NT) / tau_value))
    mate = pairs == j.astype(f32)
    live_row = across(live)
    total = jnp.sum(expo * live_row, axis=1, keepdims=True)
    share = live * jnp.sum(jnp.where(mate, live_row, 0.0), axis=1, keepdims=True)
    coef = (share / total).astype(bf16).astype(f32)
    coef_row = across(coef)
    mixing = expo * (coef * live_row + coef_row * live) - 2.0 * jnp.where(mate, share, 0.0)
    dunit = mm(mixing.astype(bf16), unit_b) * (loss_scale / tau_value)
    along = jnp.sum(unit * dunit, axis=1, keepdims=True)
    dproj = ((dunit - unit * along) * inv).astype(bf16)
    own = jnp.where(
        col_iota((16, 128)) == row_iota((16, 128)) + 4 * rank, 1.0, 0.0
    ).astype(bf16)
    dproj_own = mm(own, dproj).astype(bf16)
    dpooled = mm(dproj_own, head, NT).astype(bf16)
    mine = jnp.where(
        col_iota((16, CH)) == row_iota((16, CH)) + 12 * rank, 1.0, 0.0
    ).astype(bf16)
    pooled_mine = mm(mine, pooled, NT).astype(bf16)
    return dpooled[:4].astype(f32), mm(pooled_mine, dproj)


def top_kernel(gathered, head, slope, w_hbm, message, dpre_out, head_out, w, sem):
    section, rank, _, _, _ = position()

    @pl.when(section == 3)
    def _():
        copies = weight_copies(w_hbm, w, sem)
        for copy in copies:
            copy.start()
        dpooled, head_grad = contrast(gathered[...], head[...], rank)
        top = (dpooled / CELLS).astype(bf16).astype(f32)
        cot = jnp.broadcast_to(top[:, None, :], (4, CELLS, CH)).reshape(ROWS, CH)
        dpre = (cot * slope[...]).astype(bf16)
        dpre_out[...] = dpre
        head_out[...] = head_grad[:, 384:]
        message[128:, :] = head_grad[:, :384].astype(bf16)
        below = cot + conv_back(dpre.astype(f32), w, copies)
        message[:128, :] = below.astype(bf16)


def relay_kernel(active, arrived, slope, w_hbm, message, dpre_out, w, sem):
    @pl.when(lax.axis_index("section") == active)
    def _():
        copies = weight_copies(w_hbm, w, sem)
        for copy in copies:
            copy.start()
        cot = arrived[:128, :].astype(f32)
        dpre = (cot * slope[...]).astype(bf16)
        dpre_out[...] = dpre
        message[128:, :] = arrived[128:, :]
        below = cot + conv_back(dpre.astype(f32), w, copies)
        message[:128, :] = below.astype(bf16)


def bottom_kernel(arrived, slope, dpre3, dpre2, dpre1, dpre_out):
    section = lax.axis_index("section")
    for at, held in ((3, dpre3), (2, dpre2), (1, dpre1)):

        @pl.when(section == at)
        def _():
            pltpu.sync_copy(held, dpre_out)

    @pl.when(section == 0)
    def _():
        dpre_out[...] = (arrived[:128, :].astype(f32) * slope[...]).astype(bf16)


def last_kernel(arrived, dpre, w_hbm, head3, msg3, msg2, msg1, grads, head_out, w, held, sem):
    section = lax.axis_index("section")

    @pl.when(section == 3)
    def _():
        pltpu.sync_copy(msg3.at[pl.ds(0, 128)], grads)
        head_out[...] = head3[:12, :]

    for at, sent in ((2, msg2), (1, msg1)):

        @pl.when(section == at)
        def _():
            pltpu.sync_copy(sent.at[pl.ds(0, 128)], grads)
            pltpu.sync_copy(sent.at[pl.ds(128, 16)], held)
            head_out[...] = held[:, at * 128 : at * 128 + 128].astype(f32)[:12]

    @pl.when(section == 0)
    def _():
        copies = weight_copies(w_hbm, w, sem)
        for copy in copies:
            copy.start()
        below = arrived[:128, :].astype(f32) + conv_back(dpre[...].astype(f32), w, copies)
        grads[...] = below.astype(bf16)
        head_out[...] = arrived[128:, :128].astype(f32)[:12]


def split_kernel(saved, order, out0, out1, out2, out3):
    _, _, y, x, c = position()
    m = row_iota((CH, 1))
    q = (m * 43691) >> 19
    i = m - 12 * q
    channel = (y ^ (q & 3)) * 96 + (x ^ (q >> 3)) * 24 + (c ^ ((q >> 2) & 1)) * 12 + i
    pick = jnp.where(col_iota((CH, CH)) == channel, 1.0, 0.0).astype(bf16)
    turned = mm(pick, saved[...], NT).astype(bf16)
    for k, out in enumerate((out0, out1, out2, out3)):
        out[...] = turned[96 * k : 96 * k + 96]


def stack_kernel(*refs):
    near, far, out, scratch = refs[:4], refs[4:8], refs[8], refs[9]
    r = col_iota((48, 128))
    ph, pw = (r >> 3) & 3, r & 7
    for g in range(8):
        held = near[g][0:48, :] if g < 4 else far[g - 4][48:96, :]
        v = held.astype(f32)
        for tap in range(9):
            dh, dw = tap // 3 - 1, tap % 3 - 1
            shift = (-(8 * dh + dw)) % 128
            moved = pltpu.roll(v, shift, 1) if shift else v
            inside = (ph + dh >= 0) & (ph + dh < 4) & (pw + dw >= 0) & (pw + dw < 8)
            moved = jnp.where(inside, moved, 0.0)
            scratch[48 * tap : 48 * tap + 48, 128 * g : 128 * g + 128] = moved.astype(bf16)
    m = row_iota((448, 1))
    j = (m * 37450) >> 22
    rest = m - 112 * j
    i = (rest * 7282) >> 16
    source = jnp.where(rest < 108, (rest - 9 * i) * 48 + j * 12 + i, -1)
    pick = jnp.where(col_iota((448, 432)) == source, 1.0, 0.0).astype(bf16)
    out[...] = mm(pick, scratch[...]).astype(bf16)


def wgrad_kernel(stack, *refs):
    grads, outs = refs[:8], refs[8:]
    rows = jnp.concatenate([g[...] for g in grads], axis=0)
    total = mm(stack[...], rows)
    outs[0][...] = total[:112]
    for k in range(1, 4):
        outs[k][...] = total[112 * k : 112 * k + 112].astype(bf16)


def sum_kernel(own, part1, part2, part3, out):
    total = own[...] + part1[...].astype(f32)
    total = total + part2[...].astype(f32)
    total = total + part3[...].astype(f32)
    out[...] = total[:108].reshape(108, 1, CH)


def call(kernel, name, ins, outs, scratch=()):
    return pl.pallas_call(
        kernel,
        out_shape=outs,
        in_specs=[pl.BlockSpec(memory_space=space) for space in ins],
        out_specs=jax.tree.map(lambda _: pl.BlockSpec(memory_space=VMEM), outs),
        scratch_shapes=list(scratch),
        name=name,
    )


def sds(shape, dtype):
    return jax.ShapeDtypeStruct(shape, dtype)


def per_device(saved, kernels, head, counts, pairs, valid):
    ranks = lax.axis_size("dp")
    rows = saved.reshape(ROWS, CH)
    w_hbm = jnp.transpose(kernels[0], (1, 2, 0, 3))
    weights = [VMEM((3, 3, CH, CH), bf16), pltpu.SemaphoreType.DMA((3,))]
    act = sds((ROWS, CH), bf16)
    msg = sds((MSG, CH), bf16)

    def swap(value, bits):
        return lax.ppermute(value, "dp", [(d, d ^ bits) for d in range(ranks)])

    def relay(value, pairs_of):
        both = [(a, b) for a, b in pairs_of] + [(b, a) for a, b in pairs_of]
        return lax.ppermute(value, "section", both)

    slope, announce = call(
        forward_kernel,
        "forward",
        [VMEM, ANY, SMEM, SMEM, SMEM],
        (sds((ROWS, CH), f32), sds((256, 256), bf16)),
        weights,
    )(rows, w_hbm, counts, pairs, valid)
    gathered = lax.all_to_all(announce.reshape(32, 8, 256), "dp", 0, 0, tiled=True)
    msg3, dpre3, head3 = call(
        top_kernel,
        "top",
        [VMEM, VMEM, VMEM, ANY],
        (msg, act, sds((16, 128), f32)),
        weights,
    )(gathered.reshape(256, 256), head, slope, w_hbm)

    def relay_step(active, arrived):
        return call(
            functools.partial(relay_kernel, active),
            f"relay{active}",
            [VMEM, VMEM, ANY],
            (msg, act),
            weights,
        )(arrived, slope, w_hbm)

    arrived = relay(msg3, [(3, 2), (1, 0)])
    split = call(split_kernel, "split", [VMEM, ANY], (sds((96, 128), bf16),) * 4)(rows, msg3)
    near = [split[0]] + [swap(split[k], 2 * k) for k in range(1, 4)]
    far = [swap(value, 1) for value in near]
    stack = call(
        stack_kernel,
        "stack",
        [VMEM] * 8,
        sds((448, 1024), bf16),
        [VMEM((432, 1024), bf16)],
    )(*near, *far)

    msg2, dpre2 = relay_step(2, arrived)
    arrived = relay(msg2, [(2, 1), (3, 0)])
    msg1, dpre1 = relay_step(1, arrived)
    arrived = relay(msg1, [(1, 0), (3, 2)])
    dpre = call(bottom_kernel, "bottom", [VMEM, VMEM, ANY, ANY, ANY], act)(
        arrived, slope, dpre3, dpre2, dpre1
    )
    near_grads = [dpre] + [swap(dpre, 2 * k) for k in range(1, 4)]
    far_grads = [swap(value, 1) for value in near_grads]
    grads, head_grad = call(
        last_kernel,
        "last",
        [VMEM, VMEM, ANY, VMEM, ANY, ANY, ANY],
        (act, sds((12, 128), f32)),
        [weights[0], VMEM((16, CH), bf16), weights[1]],
    )(arrived, dpre, w_hbm, head3, msg3, msg2, msg1)
    part = sds((112, CH), bf16)
    own, *parts = call(
        wgrad_kernel, "wgrad", [VMEM] * 9, (sds((112, CH), f32), part, part, part)
    )(stack, *near_grads, *far_grads)
    parts = [swap(parts[k - 1], 8 * k) for k in range(1, 4)]
    wgrad = call(sum_kernel, "sum", [VMEM] * 4, sds((108, 1, CH), f32))(own, *parts)
    return (
        grads.reshape(saved.shape),
        wgrad.reshape(1, 12, 3, 3, CH),
        head_grad,
    )


def solution(mesh):
    return jax.shard_map(
        per_device,
        mesh=mesh,
        in_specs=(
            P("section", "dp", None, None, None),
            P("section", None, None, None, None),
            P(),
            P("dp"),
            P("dp"),
            P("dp"),
        ),
        out_specs=(
            P("section", "dp", None, None, None),
            P("section", "dp", None, None, None),
            P("dp", "section"),
        ),
        check_vma=False,
    )
```

```python
import jax
import jax.numpy as jnp
from jax import lax
from jax.experimental import pallas as pl
from jax.experimental.pallas import tpu as pltpu
from jax.sharding import PartitionSpec as P


tau_value = 0.2
loss_scale = 32.0
norm_eps = 1e-06
VMEM = pltpu.VMEM
SMEM = pltpu.SMEM
HBM = pltpu.HBM
f32 = jnp.float32
bf16 = jnp.bfloat16
NN = (((1,), (0,)), ((), ()))
NT = (((1,), (1,)), ((), ()))

ROWS, CELLS, CH, EMB = 128, 32, 384, 512
MSG = 144


def mm(a, b, dims=NN):
    return lax.dot_general(a, b, dims, preferred_element_type=f32)


def row_iota(shape):
    return lax.broadcasted_iota(jnp.int32, shape, 0)


def col_iota(shape):
    return lax.broadcasted_iota(jnp.int32, shape, 1)


def position():
    rank = lax.axis_index("dp")
    return lax.axis_index("section"), rank, (rank >> 3), ((rank >> 1) & 3), (rank & 1)


def column_shifts(v):
    pw = row_iota((ROWS, 1)) & 7
    left = jnp.where(pw > 0, pltpu.roll(v, 1, 0), 0.0)
    right = jnp.where(pw < 7, pltpu.roll(v, ROWS - 1, 0), 0.0)
    return left, v, right


def row_shift(v, dh):
    if dh == 0:
        return v
    v = v.reshape(4, CELLS, CH)
    zero = jnp.zeros((4, 8, CH), v.dtype)
    if dh > 0:
        v = jnp.concatenate([v[:, 8:], zero], axis=1)
    else:
        v = jnp.concatenate([zero, v[:, :24]], axis=1)
    return v.reshape(ROWS, CH)


def conv_back(dpre, w):
    cols = column_shifts(dpre)
    total = None
    for kh in range(3):
        lhs = jnp.concatenate(
            [row_shift(cols[2 - kw], 1 - kh).astype(bf16) for kw in range(3)], axis=1
        )
        rhs = jnp.concatenate([w[kh, kw] for kw in range(3)], axis=1)
        part = mm(lhs, rhs, NT)
        total = part if total is None else total + part
    return total


def forward_kernel(
    saved_hbm, w_hbm, head_hbm, counts, pairs, valid, slope, message, saved, w, head, sem
):
    sources = [saved_hbm, w_hbm.at[0], w_hbm.at[1], w_hbm.at[2], head_hbm]
    targets = [saved, w.at[0], w.at[1], w.at[2], head]
    copies = [
        pltpu.make_async_copy(source, target, sem.at[n])
        for n, (source, target) in enumerate(zip(sources, targets, strict=True))
    ]
    for copy in copies:
        copy.start()
    copies[0].wait()
    v = saved[...].astype(f32)
    cols = column_shifts(v)
    pre = None
    for kh in range(3):
        lhs = jnp.concatenate(
            [row_shift(cols[kw], kh - 1).astype(bf16) for kw in range(3)], axis=1
        )
        copies[1 + kh].wait()
        part = mm(lhs, w[kh].reshape(3 * CH, CH))
        pre = part if pre is None else pre + part
    sigma = jax.nn.sigmoid(pre)
    slope[...] = sigma * (1.0 + pre * (1.0 - sigma))
    feature = (v + pre * sigma).reshape(4, CELLS, CH)
    pooled = jnp.sum(feature, axis=1) / CELLS
    copies[4].wait()
    at = (row_iota((4, 128)), col_iota((4, 128)))
    extra = jnp.zeros((4, 128), f32)
    for slot in range(4):
        alive = jnp.logical_and(slot < counts[0], valid[slot] == 1)
        here = at[0] == slot
        extra = jnp.where(
            jnp.logical_and(here, at[1] == 0), jnp.where(alive, 1.0, 0.0).astype(f32), extra
        )
        extra = jnp.where(
            jnp.logical_and(here, at[1] == 1), pairs[slot].astype(f32), extra
        )
    packed = jnp.concatenate(
        [pooled[:, :256], jnp.concatenate([pooled[:, 256:], extra], axis=1)], axis=0
    )
    pair = jnp.concatenate([packed, packed], axis=0).astype(bf16)
    for at_row in range(0, 256, 16):
        message[at_row : at_row + 16, :] = pair


def contrast(gathered, head, rank):
    slot = row_iota((128, 256))
    lane = col_iota((128, 256))
    home = ((slot >> 2) << 3) + (slot & 3)
    first = mm(jnp.where(lane == home, 1.0, 0.0).astype(bf16), gathered)
    second = mm(jnp.where(lane == home + 4, 1.0, 0.0).astype(bf16), gathered)
    pooled = jnp.concatenate([first, second[:, :128]], axis=1).astype(bf16)
    live = second[:, 128:129]
    pairs = second[:, 129:130]
    proj = mm(pooled, head)
    inv = lax.rsqrt(jnp.sum(proj * proj, axis=1, keepdims=True) + norm_eps)
    unit = proj * inv
    unit_b = unit.astype(bf16)
    i = row_iota((128, 128))
    j = col_iota((128, 128))
    same = i == j

    def across(column):
        return jnp.sum(jnp.where(same, column, 0.0), axis=0, keepdims=True)

    expo = jnp.where(same, 0.0, jnp.exp(mm(unit_b, unit_b, NT) / tau_value))
    mate = pairs == j.astype(f32)
    live_row = across(live)
    total = jnp.sum(expo * live_row, axis=1, keepdims=True)
    share = live * jnp.sum(jnp.where(mate, live_row, 0.0), axis=1, keepdims=True)
    coef = (share / total).astype(bf16).astype(f32)
    coef_row = across(coef)
    mixing = expo * (coef * live_row + coef_row * live) - 2.0 * jnp.where(mate, share, 0.0)
    dunit = mm(mixing.astype(bf16), unit_b) * (loss_scale / tau_value)
    along = jnp.sum(unit * dunit, axis=1, keepdims=True)
    dproj = ((dunit - unit * along) * inv).astype(bf16)
    own = jnp.where(
        col_iota((16, 128)) == row_iota((16, 128)) + 4 * rank, 1.0, 0.0
    ).astype(bf16)
    dproj_own = mm(own, dproj).astype(bf16)
    dpooled = mm(dproj_own, head, NT).astype(bf16)
    mine = jnp.where(
        col_iota((16, CH)) == row_iota((16, CH)) + 12 * rank, 1.0, 0.0
    ).astype(bf16)
    pooled_mine = mm(mine, pooled, NT).astype(bf16)
    return dpooled[:4].astype(f32), mm(pooled_mine, dproj)


def split_saved(saved, outs):
    _, _, y, x, c = position()
    m = row_iota((CH, 1))
    q = (m * 43691) >> 19
    i = m - 12 * q
    channel = (y ^ (q & 3)) * 96 + (x ^ (q >> 3)) * 24 + (c ^ ((q >> 2) & 1)) * 12 + i
    pick = jnp.where(col_iota((CH, CH)) == channel, 1.0, 0.0).astype(bf16)
    turned = mm(pick, saved[...], NT).astype(bf16)
    for k, out in enumerate(outs):
        out[...] = turned[96 * k : 96 * k + 96]


def top_kernel(gathered, head, slope, w, saved, message, dpre_out, head_out, *split):
    section, rank, _, _, _ = position()

    @pl.when(section == 3)
    def _():
        dpooled, head_grad = contrast(gathered[...], head[...], rank)
        top = (dpooled / CELLS).astype(bf16).astype(f32)
        cot = jnp.broadcast_to(top[:, None, :], (4, CELLS, CH)).reshape(ROWS, CH)
        dpre = (cot * slope[...]).astype(bf16)
        dpre_out[...] = dpre
        head_out[...] = head_grad[:, 384:]
        message[128:, :] = head_grad[:, :384].astype(bf16)
        below = cot + conv_back(dpre.astype(f32), w)
        message[:128, :] = below.astype(bf16)

    @pl.when(section != 3)
    def _():
        split_saved(saved, split)


def relay(active, arrived, slope, w, message, dpre_out):
    @pl.when(lax.axis_index("section") == active)
    def _():
        cot = arrived[:128, :].astype(f32)
        dpre = (cot * slope[...]).astype(bf16)
        dpre_out[...] = dpre
        message[128:, :] = arrived[128:, :]
        below = cot + conv_back(dpre.astype(f32), w)
        message[:128, :] = below.astype(bf16)


def relay2_kernel(arrived, slope, w, saved, *refs):
    relay(2, arrived, slope, w, refs[4], refs[5])

    @pl.when(lax.axis_index("section") == 3)
    def _():
        split_saved(saved, refs[6:])


def relay1_kernel(arrived, slope, w, message, dpre_out):
    relay(1, arrived, slope, w, message, dpre_out)


def bottom_kernel(arrived, slope, dpre3, dpre2, dpre1, *refs):
    section = lax.axis_index("section")
    dpre_out = refs[-1]
    for at, held in ((3, dpre3), (2, dpre2), (1, dpre1)):

        @pl.when(section == at)
        def _():
            dpre_out[...] = held[...]

    @pl.when(section == 0)
    def _():
        dpre_out[...] = (arrived[:128, :].astype(f32) * slope[...]).astype(bf16)


def last_kernel(arrived, dpre, w, head3, msg3, msg2, msg1, own, grads, head_out):
    section = lax.axis_index("section")

    @pl.when(section == 3)
    def _():
        grads[...] = msg3[:128, :]
        head_out[...] = head3[:12, :]

    for at, sent in ((2, msg2), (1, msg1)):

        @pl.when(section == at)
        def _():
            grads[...] = sent[:128, :]
            head_out[...] = sent[128:, at * 128 : at * 128 + 128].astype(f32)[:12]

    @pl.when(section == 0)
    def _():
        below = arrived[:128, :].astype(f32) + conv_back(dpre[...].astype(f32), w)
        grads[...] = below.astype(bf16)
        head_out[...] = arrived[128:, :128].astype(f32)[:12]


def stack_kernel(*refs):
    near, far, out, scratch = refs[:4], refs[4:8], refs[9], refs[10]
    r = col_iota((48, 128))
    ph, pw = (r >> 3) & 3, r & 7
    for g in range(8):
        held = near[g][0:48, :] if g < 4 else far[g - 4][48:96, :]
        v = held.astype(f32)
        for tap in range(9):
            dh, dw = tap // 3 - 1, tap % 3 - 1
            shift = (-(8 * dh + dw)) % 128
            moved = pltpu.roll(v, shift, 1) if shift else v
            inside = (ph + dh >= 0) & (ph + dh < 4) & (pw + dw >= 0) & (pw + dw < 8)
            moved = jnp.where(inside, moved, 0.0)
            scratch[48 * tap : 48 * tap + 48, 128 * g : 128 * g + 128] = moved.astype(bf16)
    m = row_iota((448, 1))
    j = (m * 37450) >> 22
    rest = m - 112 * j
    i = (rest * 7282) >> 16
    source = jnp.where(rest < 108, (rest - 9 * i) * 48 + j * 12 + i, -1)
    pick = jnp.where(col_iota((448, 432)) == source, 1.0, 0.0).astype(bf16)
    out[...] = mm(pick, scratch[...]).astype(bf16)


def wgrad_kernel(stack, *refs):
    grads, outs = refs[:8], refs[8:]
    rows = jnp.concatenate([g[...] for g in grads], axis=0)
    total = mm(stack[...], rows)
    outs[0][...] = total[:112]
    for k in range(1, 4):
        outs[k][...] = total[112 * k : 112 * k + 112].astype(bf16)


def sum_kernel(own, part1, part2, part3, out):
    total = own[...] + part1[...].astype(f32)
    total = total + part2[...].astype(f32)
    total = total + part3[...].astype(f32)
    out[...] = total[:108].reshape(108, 1, CH)


def call(kernel, ins, outs, scratch=(), aliases=None):
    run = pl.pallas_call(
        kernel,
        out_shape=outs,
        in_specs=[pl.BlockSpec(memory_space=space) for space in ins],
        out_specs=jax.tree.map(
            lambda _: pl.BlockSpec(memory_space=VMEM), outs, is_leaf=lambda o: not isinstance(o, tuple)
        ),
        scratch_shapes=list(scratch),
        input_output_aliases=aliases or {},
        compiler_params=pltpu.CompilerParams(vmem_limit_bytes=24 << 20),
    )

    def with_operands(*operands):
        return run(
            *[
                value
                if space is SMEM
                else pltpu.with_memory_space_constraint(value, space)
                for value, space in zip(operands, ins, strict=True)
            ]
        )

    return with_operands


def sds(shape, dtype):
    return jax.ShapeDtypeStruct(shape, dtype)


def per_device(saved, kernels, head, counts, pairs, valid):
    ranks = lax.axis_size("dp")
    act = VMEM((ROWS, CH), bf16)
    msg = VMEM((MSG, CH), bf16)
    piece = VMEM((96, 128), bf16)

    def swap(value, bits):
        return lax.ppermute(value, "dp", [(d, d ^ bits) for d in range(ranks)])

    def relayed(value, pairs_of):
        both = [(a, b) for a, b in pairs_of] + [(b, a) for a, b in pairs_of]
        return lax.ppermute(value, "section", both)

    slope, announce, rows, w, head = call(
        forward_kernel,
        [HBM] * 3 + [SMEM] * 3,
        (
            VMEM((ROWS, CH), f32),
            VMEM((256, 256), bf16),
            act,
            VMEM((3, 3, CH, CH), bf16),
            VMEM((CH, EMB), bf16),
        ),
        [pltpu.SemaphoreType.DMA((5,))],
    )(
        saved.reshape(ROWS, CH),
        jnp.transpose(kernels[0], (1, 2, 0, 3)),
        head,
        counts,
        pairs,
        valid,
    )
    gathered = lax.all_to_all(announce.reshape(32, 8, 256), "dp", 0, 0, tiled=True)
    msg3, dpre3, head3, *split = call(
        top_kernel, [VMEM] * 5, (msg, act, VMEM((16, 128), f32)) + (piece,) * 4
    )(gathered.reshape(256, 256), head, slope, w, rows)
    arrived = relayed(msg3, [(3, 2), (1, 0)])
    msg2, dpre2, *split = call(
        relay2_kernel,
        [VMEM] * 8,
        (msg, act) + (piece,) * 4,
        aliases={4 + k: 2 + k for k in range(4)},
    )(arrived, slope, w, rows, *split)
    arrived = relayed(msg2, [(2, 1), (3, 0)])
    near = [split[0]] + [swap(split[k], 2 * k) for k in range(1, 4)]
    msg1, dpre1 = call(relay1_kernel, [VMEM] * 3, (msg, act))(arrived, slope, w)
    arrived = relayed(msg1, [(1, 0), (3, 2)])
    far = [swap(value, 1) for value in near]
    dpre = call(bottom_kernel, [VMEM] * 9, act)(
        arrived, slope, dpre3, dpre2, dpre1, *far
    )
    near_grads = [dpre] + [swap(dpre, 2 * k) for k in range(1, 4)]
    stack = call(
        stack_kernel, [VMEM] * 9, VMEM((448, 1024), bf16), [VMEM((432, 1024), bf16)]
    )(*near, *far, dpre)
    far_grads = [swap(value, 1) for value in near_grads]
    part = VMEM((112, CH), bf16)
    own, *parts = call(
        wgrad_kernel, [VMEM] * 9, (VMEM((112, CH), f32), part, part, part)
    )(stack, *near_grads, *far_grads)
    parts = [swap(parts[k - 1], 8 * k) for k in range(1, 4)]
    grads, head_grad = call(
        last_kernel, [VMEM] * 8, (sds((ROWS, CH), bf16), sds((12, 128), f32))
    )(arrived, dpre, w, head3, msg3, msg2, msg1, own)
    wgrad = call(sum_kernel, [VMEM] * 4, sds((108, 1, CH), f32))(own, *parts)
    return (
        grads.reshape(saved.shape),
        wgrad.reshape(1, 12, 3, 3, CH),
        head_grad,
    )


def solution(mesh):
    return jax.shard_map(
        per_device,
        mesh=mesh,
        in_specs=(
            P("section", "dp", None, None, None),
            P("section", None, None, None, None),
            P(),
            P("dp"),
            P("dp"),
            P("dp"),
        ),
        out_specs=(
            P("section", "dp", None, None, None),
            P("section", "dp", None, None, None),
            P("dp", "section"),
        ),
        check_vma=False,
    )
```

```python
import jax
import jax.numpy as jnp
from jax import lax
from jax.experimental import pallas as pl
from jax.experimental.pallas import tpu as pltpu
from jax.sharding import PartitionSpec as P


tau_value = 0.2
loss_scale = 32.0
norm_eps = 1e-06
VMEM = pltpu.VMEM
SMEM = pltpu.SMEM
HBM = pltpu.HBM
f32 = jnp.float32
bf16 = jnp.bfloat16
NN = (((1,), (0,)), ((), ()))
NT = (((1,), (1,)), ((), ()))

ROWS, CELLS, CH, EMB = 128, 32, 384, 512
MSG = 144


def mm(a, b, dims=NN):
    return lax.dot_general(a, b, dims, preferred_element_type=f32)


def row_iota(shape):
    return lax.broadcasted_iota(jnp.int32, shape, 0)


def col_iota(shape):
    return lax.broadcasted_iota(jnp.int32, shape, 1)


def position():
    rank = lax.axis_index("dp")
    return lax.axis_index("section"), rank, (rank >> 3), ((rank >> 1) & 3), (rank & 1)


def column_shifts(v):
    pw = row_iota((ROWS, 1)) & 7
    left = jnp.where(pw > 0, pltpu.roll(v, 1, 0), 0.0)
    right = jnp.where(pw < 7, pltpu.roll(v, ROWS - 1, 0), 0.0)
    return left, v, right


def row_shift(v, dh):
    if dh == 0:
        return v
    v = v.reshape(4, CELLS, CH)
    zero = jnp.zeros((4, 8, CH), v.dtype)
    if dh > 0:
        v = jnp.concatenate([v[:, 8:], zero], axis=1)
    else:
        v = jnp.concatenate([zero, v[:, :24]], axis=1)
    return v.reshape(ROWS, CH)


def conv_back(dpre, w):
    cols = column_shifts(dpre)
    total = None
    for kh in range(3):
        lhs = jnp.concatenate(
            [row_shift(cols[2 - kw], 1 - kh).astype(bf16) for kw in range(3)], axis=1
        )
        rhs = jnp.concatenate([w[kh, kw] for kw in range(3)], axis=1)
        part = mm(lhs, rhs, NT)
        total = part if total is None else total + part
    return total


def forward_kernel(
    saved_hbm, w_hbm, head_hbm, counts, pairs_hbm, valid_hbm,
    slope, message, saved, w, head, pairs, valid, sem,
):
    sources = [saved_hbm, w_hbm.at[0], w_hbm.at[1], w_hbm.at[2], pairs_hbm, valid_hbm, head_hbm]
    targets = [saved, w.at[0], w.at[1], w.at[2], pairs, valid, head]
    copies = [
        pltpu.make_async_copy(source, target, sem.at[n])
        for n, (source, target) in enumerate(zip(sources, targets, strict=True))
    ]
    for copy in copies:
        copy.start()
    copies[0].wait()
    v = saved[...].astype(f32)
    cols = column_shifts(v)
    pre = None
    for kh in range(3):
        lhs = jnp.concatenate(
            [row_shift(cols[kw], kh - 1).astype(bf16) for kw in range(3)], axis=1
        )
        copies[1 + kh].wait()
        part = mm(lhs, w[kh].reshape(3 * CH, CH))
        pre = part if pre is None else pre + part
    sigma = jax.nn.sigmoid(pre)
    slope[...] = sigma * (1.0 + pre * (1.0 - sigma))
    feature = (v + pre * sigma).reshape(4, CELLS, CH)
    pooled = jnp.sum(feature, axis=1) / CELLS
    for copy in copies[4:]:
        copy.wait()
    at = (row_iota((4, 128)), col_iota((4, 128)))
    extra = jnp.zeros((4, 128), f32)
    for slot in range(4):
        alive = jnp.logical_and(slot < counts[0], valid[slot] == 1)
        here = at[0] == slot
        extra = jnp.where(
            jnp.logical_and(here, at[1] == 0), jnp.where(alive, 1.0, 0.0).astype(f32), extra
        )
        extra = jnp.where(
            jnp.logical_and(here, at[1] == 1), pairs[slot].astype(f32), extra
        )
    packed = jnp.concatenate(
        [pooled[:, :256], jnp.concatenate([pooled[:, 256:], extra], axis=1)], axis=0
    )
    pair = jnp.concatenate([packed, packed], axis=0).astype(bf16)
    for at_row in range(0, 256, 16):
        message[at_row : at_row + 16, :] = pair


def contrast(gathered, head, rank):
    slot = row_iota((128, 256))
    lane = col_iota((128, 256))
    home = ((slot >> 2) << 3) + (slot & 3)
    first = mm(jnp.where(lane == home, 1.0, 0.0).astype(bf16), gathered)
    second = mm(jnp.where(lane == home + 4, 1.0, 0.0).astype(bf16), gathered)
    pooled = jnp.concatenate([first, second[:, :128]], axis=1).astype(bf16)
    live = second[:, 128:129]
    pairs = second[:, 129:130]
    proj = mm(pooled, head)
    inv = lax.rsqrt(jnp.sum(proj * proj, axis=1, keepdims=True) + norm_eps)
    unit = proj * inv
    unit_b = unit.astype(bf16)
    i = row_iota((128, 128))
    j = col_iota((128, 128))
    same = i == j

    def across(column):
        return jnp.sum(jnp.where(same, column, 0.0), axis=0, keepdims=True)

    expo = jnp.where(same, 0.0, jnp.exp(mm(unit_b, unit_b, NT) / tau_value))
    mate = pairs == j.astype(f32)
    live_row = across(live)
    total = jnp.sum(expo * live_row, axis=1, keepdims=True)
    share = live * jnp.sum(jnp.where(mate, live_row, 0.0), axis=1, keepdims=True)
    coef = (share / total).astype(bf16).astype(f32)
    coef_row = across(coef)
    mixing = expo * (coef * live_row + coef_row * live) - 2.0 * jnp.where(mate, share, 0.0)
    dunit = mm(mixing.astype(bf16), unit_b) * (loss_scale / tau_value)
    along = jnp.sum(unit * dunit, axis=1, keepdims=True)
    dproj = ((dunit - unit * along) * inv).astype(bf16)
    own = jnp.where(
        col_iota((16, 128)) == row_iota((16, 128)) + 4 * rank, 1.0, 0.0
    ).astype(bf16)
    dproj_own = mm(own, dproj).astype(bf16)
    dpooled = mm(dproj_own, head, NT).astype(bf16)
    mine = jnp.where(
        col_iota((16, CH)) == row_iota((16, CH)) + 12 * rank, 1.0, 0.0
    ).astype(bf16)
    pooled_mine = mm(mine, pooled, NT).astype(bf16)
    return dpooled[:4].astype(f32), mm(pooled_mine, dproj)


def split_kernel(saved, order, *outs):
    _, _, y, x, c = position()
    m = row_iota((CH, 1))
    q = (m * 43691) >> 19
    i = m - 12 * q
    j, k = q & 3, q >> 3
    to_y = y ^ (k >> 1) ^ (3 * (j >> 1))
    to_x = x ^ (k & 1) ^ (3 * (j & 1))
    channel = to_y * 96 + to_x * 24 + (c ^ ((q >> 2) & 1)) * 12 + i
    pick = jnp.where(col_iota((CH, CH)) == channel, 1.0, 0.0).astype(bf16)
    turned = mm(pick, saved[...], NT).astype(bf16)
    for k, out in enumerate(outs):
        out[...] = turned[96 * k : 96 * k + 96]


def top_kernel(gathered, head, slope, w, message, dpre_out, head_out):
    section, rank, _, _, _ = position()

    @pl.when(section == 3)
    def _():
        dpooled, head_grad = contrast(gathered[...], head[...], rank)
        top = (dpooled / CELLS).astype(bf16).astype(f32)
        cot = jnp.broadcast_to(top[:, None, :], (4, CELLS, CH)).reshape(ROWS, CH)
        dpre = (cot * slope[...]).astype(bf16)
        dpre_out[...] = dpre
        head_out[...] = head_grad[:, 384:]
        message[128:, :] = head_grad[:, :384].astype(bf16)
        below = cot + conv_back(dpre.astype(f32), w)
        message[:128, :] = below.astype(bf16)


def relay(active, arrived, slope, w, message, dpre_out):
    @pl.when(lax.axis_index("section") == active)
    def _():
        cot = arrived[:128, :].astype(f32)
        dpre = (cot * slope[...]).astype(bf16)
        dpre_out[...] = dpre
        message[128:, :] = arrived[128:, :]
        below = cot + conv_back(dpre.astype(f32), w)
        message[:128, :] = below.astype(bf16)


def relay2_kernel(arrived, slope, w, message, dpre_out):
    relay(2, arrived, slope, w, message, dpre_out)


def relay1_kernel(arrived, slope, w, message, dpre_out):
    relay(1, arrived, slope, w, message, dpre_out)


def bottom_kernel(arrived, slope, dpre3, dpre2, dpre1, *refs):
    section = lax.axis_index("section")
    dpre_out = refs[-1]
    for at, held in ((3, dpre3), (2, dpre2), (1, dpre1)):

        @pl.when(section == at)
        def _():
            dpre_out[...] = held[...]

    @pl.when(section == 0)
    def _():
        dpre_out[...] = (arrived[:128, :].astype(f32) * slope[...]).astype(bf16)


def last_kernel(arrived, dpre, w, head3, msg3, msg2, msg1, own, grads, head_out):
    section = lax.axis_index("section")

    @pl.when(section == 3)
    def _():
        grads[...] = msg3[:128, :]
        head_out[...] = head3[:12, :]

    for at, sent in ((2, msg2), (1, msg1)):

        @pl.when(section == at)
        def _():
            grads[...] = sent[:128, :]
            head_out[...] = sent[128:, at * 128 : at * 128 + 128].astype(f32)[:12]

    @pl.when(section == 0)
    def _():
        below = arrived[:128, :].astype(f32) + conv_back(dpre[...].astype(f32), w)
        grads[...] = below.astype(bf16)
        head_out[...] = arrived[128:, :128].astype(f32)[:12]


def stack_kernel(*refs):
    near, far, out, scratch = refs[:4], refs[4:8], refs[9], refs[10]
    r = col_iota((48, 128))
    ph, pw = (r >> 3) & 3, r & 7
    for g in range(8):
        held = near[g][0:48, :] if g < 4 else far[g - 4][48:96, :]
        v = held.astype(f32)
        for tap in range(9):
            dh, dw = tap // 3 - 1, tap % 3 - 1
            shift = (-(8 * dh + dw)) % 128
            moved = pltpu.roll(v, shift, 1) if shift else v
            inside = (ph + dh >= 0) & (ph + dh < 4) & (pw + dw >= 0) & (pw + dw < 8)
            moved = jnp.where(inside, moved, 0.0)
            scratch[48 * tap : 48 * tap + 48, 128 * g : 128 * g + 128] = moved.astype(bf16)
    m = row_iota((448, 1))
    j = (m * 37450) >> 22
    rest = m - 112 * j
    i = (rest * 7282) >> 16
    source = jnp.where(rest < 108, (rest - 9 * i) * 48 + j * 12 + i, -1)
    pick = jnp.where(col_iota((448, 432)) == source, 1.0, 0.0).astype(bf16)
    out[...] = mm(pick, scratch[...]).astype(bf16)


def wgrad_kernel(stack, *refs):
    grads, outs = refs[:8], refs[8:]
    rows = jnp.concatenate([g[...] for g in grads], axis=0)
    total = mm(stack[...], rows)
    outs[0][...] = total[:112]
    for k in range(1, 4):
        outs[k][...] = total[112 * k : 112 * k + 112].astype(bf16)


def sum_kernel(own, part1, part2, part3, out):
    total = own[...] + part1[...].astype(f32)
    total = total + part2[...].astype(f32)
    total = total + part3[...].astype(f32)
    out[...] = total[:108].reshape(108, 1, CH)


def call(kernel, ins, outs, scratch=(), aliases=None):
    run = pl.pallas_call(
        kernel,
        out_shape=outs,
        in_specs=[pl.BlockSpec(memory_space=space) for space in ins],
        out_specs=jax.tree.map(
            lambda _: pl.BlockSpec(memory_space=VMEM), outs, is_leaf=lambda o: not isinstance(o, tuple)
        ),
        scratch_shapes=list(scratch),
        input_output_aliases=aliases or {},
        compiler_params=pltpu.CompilerParams(vmem_limit_bytes=24 << 20),
    )

    def with_operands(*operands):
        return run(
            *[
                value
                if space is SMEM
                else pltpu.with_memory_space_constraint(value, space)
                for value, space in zip(operands, ins, strict=True)
            ]
        )

    return with_operands


def sds(shape, dtype):
    return jax.ShapeDtypeStruct(shape, dtype)


def per_device(saved, kernels, head, counts, pairs, valid):
    ranks = lax.axis_size("dp")
    act = VMEM((ROWS, CH), bf16)
    msg = VMEM((MSG, CH), bf16)
    piece = VMEM((96, 128), bf16)
    gather = (0, 2, 8, 10)
    reduce = (0, 6, 24, 30)

    def swap(value, bits):
        return lax.ppermute(value, "dp", [(d, d ^ bits) for d in range(ranks)])

    def relayed(value, pairs_of):
        both = [(a, b) for a, b in pairs_of] + [(b, a) for a, b in pairs_of]
        return lax.ppermute(value, "section", both)

    slope, announce, rows, w, head = call(
        forward_kernel,
        [HBM] * 3 + [SMEM] + [HBM] * 2,
        (
            VMEM((ROWS, CH), f32),
            VMEM((256, 256), bf16),
            act,
            VMEM((3, 3, CH, CH), bf16),
            VMEM((CH, EMB), bf16),
        ),
        [SMEM((4,), jnp.int32), SMEM((4,), jnp.int32), pltpu.SemaphoreType.DMA((7,))],
    )(
        saved.reshape(ROWS, CH),
        jnp.transpose(kernels[0], (1, 2, 0, 3)),
        head,
        counts,
        pairs,
        valid,
    )
    gathered = lax.all_to_all(announce.reshape(32, 8, 256), "dp", 0, 0, tiled=True)
    msg3, dpre3, head3 = call(
        top_kernel, [VMEM] * 4, (msg, act, VMEM((16, 128), f32))
    )(gathered.reshape(256, 256), head, slope, w)
    arrived = relayed(msg3, [(3, 2), (1, 0)])
    split = call(split_kernel, [VMEM] * 2, (piece,) * 4)(rows, msg3)
    near = [split[0]] + [swap(split[k], gather[k]) for k in range(1, 4)]
    msg2, dpre2 = call(relay2_kernel, [VMEM] * 3, (msg, act))(arrived, slope, w)
    arrived = relayed(msg2, [(2, 1), (3, 0)])
    msg1, dpre1 = call(relay1_kernel, [VMEM] * 3, (msg, act))(arrived, slope, w)
    arrived = relayed(msg1, [(1, 0), (3, 2)])
    far = [swap(value, 1) for value in near]
    dpre = call(bottom_kernel, [VMEM] * 9, act)(
        arrived, slope, dpre3, dpre2, dpre1, *far
    )
    near_grads = [dpre] + [swap(dpre, gather[k]) for k in range(1, 4)]
    stack = call(
        stack_kernel, [VMEM] * 9, VMEM((448, 1024), bf16), [VMEM((432, 1024), bf16)]
    )(*near, *far, dpre)
    far_grads = [swap(value, 1) for value in near_grads]
    part = VMEM((112, CH), bf16)
    own, *parts = call(
        wgrad_kernel, [VMEM] * 9, (VMEM((112, CH), f32), part, part, part)
    )(stack, *near_grads, *far_grads)
    parts = [swap(parts[k - 1], reduce[k]) for k in range(1, 4)]
    grads, head_grad = call(
        last_kernel, [VMEM] * 8, (sds((ROWS, CH), bf16), sds((12, 128), f32))
    )(arrived, dpre, w, head3, msg3, msg2, msg1, own)
    wgrad = call(sum_kernel, [VMEM] * 4, sds((108, 1, CH), f32))(own, *parts)
    return (
        grads.reshape(saved.shape),
        wgrad.reshape(1, 12, 3, 3, CH),
        head_grad,
    )


def solution(mesh):
    return jax.shard_map(
        per_device,
        mesh=mesh,
        in_specs=(
            P("section", "dp", None, None, None),
            P("section", None, None, None, None),
            P(),
            P("dp"),
            P("dp"),
            P("dp"),
        ),
        out_specs=(
            P("section", "dp", None, None, None),
            P("section", "dp", None, None, None),
            P("dp", "section"),
        ),
        check_vma=False,
    )
```

```python
import jax
import jax.numpy as jnp
from jax import lax
from jax.experimental import pallas as pl
from jax.experimental.pallas import tpu as pltpu
from jax.sharding import PartitionSpec as P


tau_value = 0.2
loss_scale = 32.0
norm_eps = 1e-06
VMEM = pltpu.VMEM
SMEM = pltpu.SMEM
HBM = pltpu.HBM
f32 = jnp.float32
bf16 = jnp.bfloat16
NN = (((1,), (0,)), ((), ()))
NT = (((1,), (1,)), ((), ()))

ROWS, CELLS, CH, EMB = 128, 32, 384, 512
MSG = 144


def mm(a, b, dims=NN):
    return lax.dot_general(a, b, dims, preferred_element_type=f32)


def row_iota(shape):
    return lax.broadcasted_iota(jnp.int32, shape, 0)


def col_iota(shape):
    return lax.broadcasted_iota(jnp.int32, shape, 1)


def position():
    rank = lax.axis_index("dp")
    return lax.axis_index("section"), rank, (rank >> 3), ((rank >> 1) & 3), (rank & 1)


def column_shifts(v):
    pw = row_iota((ROWS, 1)) & 7
    left = jnp.where(pw > 0, pltpu.roll(v, 1, 0), 0.0)
    right = jnp.where(pw < 7, pltpu.roll(v, ROWS - 1, 0), 0.0)
    return left, v, right


def row_shift(v, dh):
    if dh == 0:
        return v
    v = v.reshape(4, CELLS, CH)
    zero = jnp.zeros((4, 8, CH), v.dtype)
    if dh > 0:
        v = jnp.concatenate([v[:, 8:], zero], axis=1)
    else:
        v = jnp.concatenate([zero, v[:, :24]], axis=1)
    return v.reshape(ROWS, CH)


def conv_back(dpre, w):
    cols = column_shifts(dpre)
    total = None
    for kh in range(3):
        lhs = jnp.concatenate(
            [row_shift(cols[2 - kw], 1 - kh).astype(bf16) for kw in range(3)], axis=1
        )
        rhs = jnp.concatenate([w[kh, kw] for kw in range(3)], axis=1)
        part = mm(lhs, rhs, NT)
        total = part if total is None else total + part
    return total


def forward_kernel(
    saved_hbm, w_hbm, head_hbm, counts, pairs_hbm, valid_hbm,
    slope, message, saved, w, head, pairs, valid, sem,
):
    sources = [saved_hbm, w_hbm.at[0], w_hbm.at[1], w_hbm.at[2], pairs_hbm, valid_hbm, head_hbm]
    targets = [saved, w.at[0], w.at[1], w.at[2], pairs, valid, head]
    copies = [
        pltpu.make_async_copy(source, target, sem.at[n])
        for n, (source, target) in enumerate(zip(sources, targets, strict=True))
    ]
    for copy in copies:
        copy.start()
    copies[0].wait()
    v = saved[...].astype(f32)
    cols = column_shifts(v)
    pre = None
    for kh in range(3):
        lhs = jnp.concatenate(
            [row_shift(cols[kw], kh - 1).astype(bf16) for kw in range(3)], axis=1
        )
        copies[1 + kh].wait()
        part = mm(lhs, w[kh].reshape(3 * CH, CH))
        pre = part if pre is None else pre + part
    sigma = jax.nn.sigmoid(pre)
    slope[...] = sigma * (1.0 + pre * (1.0 - sigma))
    feature = (v + pre * sigma).reshape(4, CELLS, CH)
    pooled = jnp.sum(feature, axis=1) / CELLS
    for copy in copies[4:]:
        copy.wait()
    at = (row_iota((4, 128)), col_iota((4, 128)))
    extra = jnp.zeros((4, 128), f32)
    for slot in range(4):
        alive = jnp.logical_and(slot < counts[0], valid[slot] == 1)
        here = at[0] == slot
        extra = jnp.where(
            jnp.logical_and(here, at[1] == 0), jnp.where(alive, 1.0, 0.0).astype(f32), extra
        )
        extra = jnp.where(
            jnp.logical_and(here, at[1] == 1), pairs[slot].astype(f32), extra
        )
    packed = jnp.concatenate(
        [pooled[:, :256], jnp.concatenate([pooled[:, 256:], extra], axis=1)], axis=0
    )
    pair = jnp.concatenate([packed, packed], axis=0).astype(bf16)
    for at_row in range(0, 256, 16):
        message[at_row : at_row + 16, :] = pair


def contrast(gathered, head, rank):
    slot = row_iota((128, 256))
    lane = col_iota((128, 256))
    home = ((slot >> 2) << 3) + (slot & 3)
    first = mm(jnp.where(lane == home, 1.0, 0.0).astype(bf16), gathered)
    second = mm(jnp.where(lane == home + 4, 1.0, 0.0).astype(bf16), gathered)
    pooled = jnp.concatenate([first, second[:, :128]], axis=1).astype(bf16)
    live = second[:, 128:129]
    pairs = second[:, 129:130]
    proj = mm(pooled, head)
    inv = lax.rsqrt(jnp.sum(proj * proj, axis=1, keepdims=True) + norm_eps)
    unit = proj * inv
    unit_b = unit.astype(bf16)
    i = row_iota((128, 128))
    j = col_iota((128, 128))
    same = i == j

    def across(column):
        return jnp.sum(jnp.where(same, column, 0.0), axis=0, keepdims=True)

    expo = jnp.where(same, 0.0, jnp.exp(mm(unit_b, unit_b, NT) / tau_value))
    mate = pairs == j.astype(f32)
    live_row = across(live)
    total = jnp.sum(expo * live_row, axis=1, keepdims=True)
    share = live * jnp.sum(jnp.where(mate, live_row, 0.0), axis=1, keepdims=True)
    coef = (share / total).astype(bf16).astype(f32)
    coef_row = across(coef)
    mixing = expo * (coef * live_row + coef_row * live) - 2.0 * jnp.where(mate, share, 0.0)
    dunit = mm(mixing.astype(bf16), unit_b) * (loss_scale / tau_value)
    along = jnp.sum(unit * dunit, axis=1, keepdims=True)
    dproj = ((dunit - unit * along) * inv).astype(bf16)
    own = jnp.where(
        col_iota((16, 128)) == row_iota((16, 128)) + 4 * rank, 1.0, 0.0
    ).astype(bf16)
    dproj_own = mm(own, dproj).astype(bf16)
    dpooled = mm(dproj_own, head, NT).astype(bf16)
    mine = jnp.where(
        col_iota((16, CH)) == row_iota((16, CH)) + 12 * rank, 1.0, 0.0
    ).astype(bf16)
    pooled_mine = mm(mine, pooled, NT).astype(bf16)
    return dpooled[:4].astype(f32), mm(pooled_mine, dproj)


def split_kernel(saved, order, *outs):
    _, _, y, x, c = position()
    m = row_iota((CH, 1))
    q = (m * 43691) >> 19
    i = m - 12 * q
    j, k = q & 3, q >> 3
    core = c ^ ((q >> 2) & 1)
    flip_x = jnp.where((j == 3) | ((j > 0) & (core == 0)), 3, 0)
    flip_y = jnp.where((j == 3) | ((j > 0) & (core == 1)), 3, 0)
    to_y = y ^ (k >> 1) ^ flip_y
    to_x = x ^ (k & 1) ^ flip_x
    to_core = core ^ jnp.where(j == 2, 1, 0)
    channel = to_y * 96 + to_x * 24 + to_core * 12 + i
    pick = jnp.where(col_iota((CH, CH)) == channel, 1.0, 0.0).astype(bf16)
    turned = mm(pick, saved[...], NT).astype(bf16)
    for k, out in enumerate(outs):
        out[...] = turned[96 * k : 96 * k + 96]


def top_kernel(gathered, head, slope, w, message, dpre_out, head_out):
    section, rank, _, _, _ = position()

    @pl.when(section == 3)
    def _():
        dpooled, head_grad = contrast(gathered[...], head[...], rank)
        top = (dpooled / CELLS).astype(bf16).astype(f32)
        cot = jnp.broadcast_to(top[:, None, :], (4, CELLS, CH)).reshape(ROWS, CH)
        dpre = (cot * slope[...]).astype(bf16)
        dpre_out[...] = dpre
        head_out[...] = head_grad[:, 384:]
        message[128:, :] = head_grad[:, :384].astype(bf16)
        below = cot + conv_back(dpre.astype(f32), w)
        message[:128, :] = below.astype(bf16)


def relay(active, arrived, slope, w, message, dpre_out):
    @pl.when(lax.axis_index("section") == active)
    def _():
        cot = arrived[:128, :].astype(f32)
        dpre = (cot * slope[...]).astype(bf16)
        dpre_out[...] = dpre
        message[128:, :] = arrived[128:, :]
        below = cot + conv_back(dpre.astype(f32), w)
        message[:128, :] = below.astype(bf16)


def relay2_kernel(arrived, slope, w, message, dpre_out):
    relay(2, arrived, slope, w, message, dpre_out)


def relay1_kernel(arrived, slope, w, message, dpre_out):
    relay(1, arrived, slope, w, message, dpre_out)


def bottom_kernel(arrived, slope, dpre3, dpre2, dpre1, *refs):
    section = lax.axis_index("section")
    dpre_out = refs[-1]
    for at, held in ((3, dpre3), (2, dpre2), (1, dpre1)):

        @pl.when(section == at)
        def _():
            dpre_out[...] = held[...]

    @pl.when(section == 0)
    def _():
        dpre_out[...] = (arrived[:128, :].astype(f32) * slope[...]).astype(bf16)


def last_kernel(arrived, dpre, w, head3, msg3, msg2, msg1, own, grads, head_out):
    section = lax.axis_index("section")

    @pl.when(section == 3)
    def _():
        grads[...] = msg3[:128, :]
        head_out[...] = head3[:12, :]

    for at, sent in ((2, msg2), (1, msg1)):

        @pl.when(section == at)
        def _():
            grads[...] = sent[:128, :]
            head_out[...] = sent[128:, at * 128 : at * 128 + 128].astype(f32)[:12]

    @pl.when(section == 0)
    def _():
        below = arrived[:128, :].astype(f32) + conv_back(dpre[...].astype(f32), w)
        grads[...] = below.astype(bf16)
        head_out[...] = arrived[128:, :128].astype(f32)[:12]


def stack_kernel(*refs):
    near, far, out, scratch = refs[:4], refs[4:8], refs[9], refs[10]
    r = col_iota((48, 128))
    ph, pw = (r >> 3) & 3, r & 7
    for g in range(8):
        held = near[g][0:48, :] if g < 4 else far[g - 4][48:96, :]
        v = held.astype(f32)
        for tap in range(9):
            dh, dw = tap // 3 - 1, tap % 3 - 1
            shift = (-(8 * dh + dw)) % 128
            moved = pltpu.roll(v, shift, 1) if shift else v
            inside = (ph + dh >= 0) & (ph + dh < 4) & (pw + dw >= 0) & (pw + dw < 8)
            moved = jnp.where(inside, moved, 0.0)
            scratch[48 * tap : 48 * tap + 48, 128 * g : 128 * g + 128] = moved.astype(bf16)
    m = row_iota((448, 1))
    j = (m * 37450) >> 22
    rest = m - 112 * j
    i = (rest * 7282) >> 16
    source = jnp.where(rest < 108, (rest - 9 * i) * 48 + j * 12 + i, -1)
    pick = jnp.where(col_iota((448, 432)) == source, 1.0, 0.0).astype(bf16)
    out[...] = mm(pick, scratch[...]).astype(bf16)


def wgrad_kernel(stack, *refs):
    grads, outs = refs[:8], refs[8:]
    rows = jnp.concatenate([g[...] for g in grads], axis=0)
    total = mm(stack[...], rows)
    outs[0][...] = total[:112]
    outs[1][...] = total[112:336].astype(bf16)
    outs[2][...] = total[336:].astype(bf16)


def sum_kernel(own, pair, crossed, diagonal, out):
    total = own[...] + pair[:112, :].astype(f32)
    total = total + crossed[112:, :].astype(f32)
    total = total + diagonal[...].astype(f32)
    out[...] = total[:108].reshape(108, 1, CH)


def call(kernel, ins, outs, scratch=(), aliases=None):
    run = pl.pallas_call(
        kernel,
        out_shape=outs,
        in_specs=[pl.BlockSpec(memory_space=space) for space in ins],
        out_specs=jax.tree.map(
            lambda _: pl.BlockSpec(memory_space=VMEM), outs, is_leaf=lambda o: not isinstance(o, tuple)
        ),
        scratch_shapes=list(scratch),
        input_output_aliases=aliases or {},
        compiler_params=pltpu.CompilerParams(vmem_limit_bytes=24 << 20),
    )

    def with_operands(*operands):
        return run(
            *[
                value
                if space is SMEM
                else pltpu.with_memory_space_constraint(value, space)
                for value, space in zip(operands, ins, strict=True)
            ]
        )

    return with_operands


def sds(shape, dtype):
    return jax.ShapeDtypeStruct(shape, dtype)


def per_device(saved, kernels, head, counts, pairs, valid):
    ranks = lax.axis_size("dp")
    act = VMEM((ROWS, CH), bf16)
    msg = VMEM((MSG, CH), bf16)
    piece = VMEM((96, 128), bf16)
    gather = (0, 2, 8, 10)

    def swap(value, bits, odd_bits=None):
        pairs_of = [(d, d ^ (odd_bits if odd_bits and d & 1 else bits)) for d in range(ranks)]
        return lax.ppermute(value, "dp", pairs_of)

    def relayed(value, pairs_of):
        both = [(a, b) for a, b in pairs_of] + [(b, a) for a, b in pairs_of]
        return lax.ppermute(value, "section", both)

    slope, announce, rows, w, head = call(
        forward_kernel,
        [HBM] * 3 + [SMEM] + [HBM] * 2,
        (
            VMEM((ROWS, CH), f32),
            VMEM((256, 256), bf16),
            act,
            VMEM((3, 3, CH, CH), bf16),
            VMEM((CH, EMB), bf16),
        ),
        [SMEM((4,), jnp.int32), SMEM((4,), jnp.int32), pltpu.SemaphoreType.DMA((7,))],
    )(
        saved.reshape(ROWS, CH),
        jnp.transpose(kernels[0], (1, 2, 0, 3)),
        head,
        counts,
        pairs,
        valid,
    )
    gathered = lax.all_to_all(announce.reshape(32, 8, 256), "dp", 0, 0, tiled=True)
    msg3, dpre3, head3 = call(
        top_kernel, [VMEM] * 4, (msg, act, VMEM((16, 128), f32))
    )(gathered.reshape(256, 256), head, slope, w)
    arrived = relayed(msg3, [(3, 2), (1, 0)])
    split = call(split_kernel, [VMEM] * 2, (piece,) * 4)(rows, msg3)
    near = [split[0]] + [swap(split[k], gather[k]) for k in range(1, 4)]
    msg2, dpre2 = call(relay2_kernel, [VMEM] * 3, (msg, act))(arrived, slope, w)
    arrived = relayed(msg2, [(2, 1), (3, 0)])
    msg1, dpre1 = call(relay1_kernel, [VMEM] * 3, (msg, act))(arrived, slope, w)
    arrived = relayed(msg1, [(1, 0), (3, 2)])
    far = [swap(value, 1) for value in near]
    dpre = call(bottom_kernel, [VMEM] * 9, act)(
        arrived, slope, dpre3, dpre2, dpre1, *far
    )
    near_grads = [dpre] + [swap(dpre, gather[k]) for k in range(1, 4)]
    stack = call(
        stack_kernel, [VMEM] * 9, VMEM((448, 1024), bf16), [VMEM((432, 1024), bf16)]
    )(*near, *far, dpre)
    far_grads = [swap(value, 1) for value in near_grads]
    own, pair, diagonal = call(
        wgrad_kernel,
        [VMEM] * 9,
        (VMEM((112, CH), f32), VMEM((224, CH), bf16), VMEM((112, CH), bf16)),
    )(stack, *near_grads, *far_grads)
    pair = swap(pair, 6, 24)
    diagonal = swap(diagonal, 30)
    crossed = swap(pair, 1)
    grads, head_grad = call(
        last_kernel, [VMEM] * 8, (sds((ROWS, CH), bf16), sds((12, 128), f32))
    )(arrived, dpre, w, head3, msg3, msg2, msg1, own)
    wgrad = call(sum_kernel, [VMEM] * 4, sds((108, 1, CH), f32))(own, pair, crossed, diagonal)
    return (
        grads.reshape(saved.shape),
        wgrad.reshape(1, 12, 3, 3, CH),
        head_grad,
    )


def solution(mesh):
    return jax.shard_map(
        per_device,
        mesh=mesh,
        in_specs=(
            P("section", "dp", None, None, None),
            P("section", None, None, None, None),
            P(),
            P("dp"),
            P("dp"),
            P("dp"),
        ),
        out_specs=(
            P("section", "dp", None, None, None),
            P("section", "dp", None, None, None),
            P("dp", "section"),
        ),
        check_vma=False,
    )
```

```python
import functools

import jax
import jax.numpy as jnp
from jax import lax
from jax.experimental import pallas as pl
from jax.experimental.pallas import tpu as pltpu
from jax.sharding import PartitionSpec as P


tau_value = 0.2
loss_scale = 32.0
norm_eps = 1e-06
VMEM = pltpu.VMEM
SMEM = pltpu.SMEM
HBM = pltpu.HBM
f32 = jnp.float32
bf16 = jnp.bfloat16
NN = (((1,), (0,)), ((), ()))
NT = (((1,), (1,)), ((), ()))

ROWS, CELLS, CH, EMB = 128, 32, 384, 512
HALF = 64


def mm(a, b, dims=NN):
    return lax.dot_general(a, b, dims, preferred_element_type=f32)


def row_iota(shape):
    return lax.broadcasted_iota(jnp.int32, shape, 0)


def col_iota(shape):
    return lax.broadcasted_iota(jnp.int32, shape, 1)


def position():
    rank = lax.axis_index("dp")
    return lax.axis_index("section"), rank, (rank >> 3), ((rank >> 1) & 3), (rank & 1)


def column_shifts(v):
    rows = v.shape[0]
    pw = row_iota((rows, 1)) & 7
    left = jnp.where(pw > 0, pltpu.roll(v, 1, 0), 0.0)
    right = jnp.where(pw < 7, pltpu.roll(v, rows - 1, 0), 0.0)
    return left, v, right


def row_shift(v, dh):
    if dh == 0:
        return v
    rows = v.shape[0]
    v = v.reshape(rows // CELLS, CELLS, CH)
    zero = jnp.zeros((rows // CELLS, 8, CH), v.dtype)
    if dh > 0:
        v = jnp.concatenate([v[:, 8:], zero], axis=1)
    else:
        v = jnp.concatenate([zero, v[:, :24]], axis=1)
    return v.reshape(rows, CH)


def conv_back(dpre, w):
    cols = column_shifts(dpre)
    total = None
    for kh in range(3):
        lhs = jnp.concatenate(
            [row_shift(cols[2 - kw], 1 - kh).astype(bf16) for kw in range(3)], axis=1
        )
        rhs = jnp.concatenate([w[kh, kw] for kw in range(3)], axis=1)
        part = mm(lhs, rhs, NT)
        total = part if total is None else total + part
    return total


def forward_kernel(
    saved_hbm, w_hbm, head_hbm, counts, pairs_hbm, valid_hbm,
    slope, message, saved, w, head, pairs, valid, sem,
):
    sources = [saved_hbm, w_hbm.at[0], w_hbm.at[1], w_hbm.at[2], pairs_hbm, valid_hbm, head_hbm]
    targets = [saved, w.at[0], w.at[1], w.at[2], pairs, valid, head]
    copies = [
        pltpu.make_async_copy(source, target, sem.at[n])
        for n, (source, target) in enumerate(zip(sources, targets, strict=True))
    ]
    for copy in copies:
        copy.start()
    copies[0].wait()
    v = saved[...].astype(f32)
    cols = column_shifts(v)
    pre = None
    for kh in range(3):
        lhs = jnp.concatenate(
            [row_shift(cols[kw], kh - 1).astype(bf16) for kw in range(3)], axis=1
        )
        copies[1 + kh].wait()
        part = mm(lhs, w[kh].reshape(3 * CH, CH))
        pre = part if pre is None else pre + part
    sigma = jax.nn.sigmoid(pre)
    slope[...] = sigma * (1.0 + pre * (1.0 - sigma))
    feature = (v + pre * sigma).reshape(4, CELLS, CH)
    pooled = jnp.sum(feature, axis=1) / CELLS
    for copy in copies[4:]:
        copy.wait()
    at = (row_iota((4, 128)), col_iota((4, 128)))
    extra = jnp.zeros((4, 128), f32)
    for slot in range(4):
        alive = jnp.logical_and(slot < counts[0], valid[slot] == 1)
        here = at[0] == slot
        extra = jnp.where(
            jnp.logical_and(here, at[1] == 0), jnp.where(alive, 1.0, 0.0).astype(f32), extra
        )
        extra = jnp.where(
            jnp.logical_and(here, at[1] == 1), pairs[slot].astype(f32), extra
        )
    packed = jnp.concatenate(
        [pooled[:, :256], jnp.concatenate([pooled[:, 256:], extra], axis=1)], axis=0
    )
    pair = jnp.concatenate([packed, packed], axis=0).astype(bf16)
    for at_row in range(0, 256, 16):
        message[at_row : at_row + 16, :] = pair


def contrast(gathered, head, rank):
    slot = row_iota((128, 256))
    lane = col_iota((128, 256))
    home = ((slot >> 2) << 3) + (slot & 3)
    first = mm(jnp.where(lane == home, 1.0, 0.0).astype(bf16), gathered)
    second = mm(jnp.where(lane == home + 4, 1.0, 0.0).astype(bf16), gathered)
    pooled = jnp.concatenate([first, second[:, :128]], axis=1).astype(bf16)
    live = second[:, 128:129]
    pairs = second[:, 129:130]
    proj = mm(pooled, head)
    inv = lax.rsqrt(jnp.sum(proj * proj, axis=1, keepdims=True) + norm_eps)
    unit = proj * inv
    unit_b = unit.astype(bf16)
    i = row_iota((128, 128))
    j = col_iota((128, 128))
    same = i == j

    def across(column):
        return jnp.sum(jnp.where(same, column, 0.0), axis=0, keepdims=True)

    expo = jnp.where(same, 0.0, jnp.exp(mm(unit_b, unit_b, NT) / tau_value))
    mate = pairs == j.astype(f32)
    live_row = across(live)
    total = jnp.sum(expo * live_row, axis=1, keepdims=True)
    share = live * jnp.sum(jnp.where(mate, live_row, 0.0), axis=1, keepdims=True)
    coef = (share / total).astype(bf16).astype(f32)
    coef_row = across(coef)
    mixing = expo * (coef * live_row + coef_row * live) - 2.0 * jnp.where(mate, share, 0.0)
    dunit = mm(mixing.astype(bf16), unit_b) * (loss_scale / tau_value)
    along = jnp.sum(unit * dunit, axis=1, keepdims=True)
    dproj = ((dunit - unit * along) * inv).astype(bf16)
    own = jnp.where(
        col_iota((16, 128)) == row_iota((16, 128)) + 4 * rank, 1.0, 0.0
    ).astype(bf16)
    dproj_own = mm(own, dproj).astype(bf16)
    dpooled = mm(dproj_own, head, NT).astype(bf16)
    mine = jnp.where(
        col_iota((16, CH)) == row_iota((16, CH)) + 12 * rank, 1.0, 0.0
    ).astype(bf16)
    pooled_mine = mm(mine, pooled, NT).astype(bf16)
    return dpooled[:4].astype(f32), mm(pooled_mine, dproj)


def split_kernel(saved, order, *outs):
    _, _, y, x, c = position()
    m = row_iota((CH, 1))
    q = (m * 43691) >> 19
    i = m - 12 * q
    j, k = q & 3, q >> 3
    core = c ^ ((q >> 2) & 1)
    flip_x = jnp.where((j == 3) | ((j > 0) & (core == 0)), 3, 0)
    flip_y = jnp.where((j == 3) | ((j > 0) & (core == 1)), 3, 0)
    to_y = y ^ (k >> 1) ^ flip_y
    to_x = x ^ (k & 1) ^ flip_x
    to_core = core ^ jnp.where(j == 2, 1, 0)
    channel = to_y * 96 + to_x * 24 + to_core * 12 + i
    pick = jnp.where(col_iota((CH, CH)) == channel, 1.0, 0.0).astype(bf16)
    turned = mm(pick, saved[...], NT).astype(bf16)
    for k, out in enumerate(outs):
        out[...] = turned[96 * k : 96 * k + 96]


def top_a_kernel(gathered, head, slope, w, message, dpre_out, head_out, top_out):
    section, rank, _, _, _ = position()

    @pl.when(section == 3)
    def _():
        dpooled, head_grad = contrast(gathered[...], head[...], rank)
        top = (dpooled / CELLS).astype(bf16).astype(f32)
        cot = jnp.broadcast_to(top[:, None, :], (4, CELLS, CH)).reshape(ROWS, CH)
        dpre = (cot * slope[...]).astype(bf16)
        dpre_out[...] = dpre
        head_out[...] = head_grad
        top_out[0:4, :] = top
        below = cot[:HALF] + conv_back(dpre[:HALF].astype(f32), w)
        message[...] = below.astype(bf16)


def top_b_kernel(top, dpre, head_grad, w, message):
    @pl.when(lax.axis_index("section") == 3)
    def _():
        cot = jnp.broadcast_to(top[2:4, :][:, None, :], (2, CELLS, CH)).reshape(HALF, CH)
        below = cot + conv_back(dpre[HALF:, :].astype(f32), w)
        message[:HALF, :] = below.astype(bf16)
        message[HALF:, :] = head_grad[:, :384].astype(bf16)


def relay_kernel(active, half, arrived, slope, w, message, dpre_out):
    @pl.when(lax.axis_index("section") == active)
    def _():
        cot = arrived[:HALF, :].astype(f32)
        dpre = (cot * slope[HALF * half : HALF * half + HALF, :]).astype(bf16)
        dpre_out[...] = dpre
        below = cot + conv_back(dpre.astype(f32), w)
        message[:HALF, :] = below.astype(bf16)
        if half:
            message[HALF:, :] = arrived[HALF:, :]


def bottom_kernel(*refs):
    arrived, slope, dpre3, held2, held1, dpre_out = (
        refs[0:2], refs[2], refs[3], refs[4:6], refs[6:8], refs[8]
    )
    section = lax.axis_index("section")

    @pl.when(section == 3)
    def _():
        dpre_out[...] = dpre3[...]

    for half in range(2):
        rows = slice(HALF * half, HALF * half + HALF)
        for at, held in ((2, held2), (1, held1)):

            @pl.when(section == at)
            def _():
                dpre_out[rows, :] = held[half][...]

        @pl.when(section == 0)
        def _():
            cot = arrived[half][:HALF, :].astype(f32)
            dpre_out[rows, :] = (cot * slope[rows, :]).astype(bf16)


def last_kernel(*refs):
    arrived, dpre, w, head3, sent, grads, head_out = (
        refs[0:2], refs[2], refs[3], refs[4], refs[5:11], refs[12], refs[13]
    )
    section = lax.axis_index("section")
    for at in (3, 2, 1):

        @pl.when(section == at)
        def _():
            first, second = sent[6 - 2 * at], sent[7 - 2 * at]
            grads[:HALF, :] = first[...]
            grads[HALF:, :] = second[:HALF, :]
            if at == 3:
                head_out[...] = head3[:12, 384:]
            else:
                head_out[...] = second[HALF:, at * 128 : at * 128 + 128].astype(f32)[:12]

    @pl.when(section == 0)
    def _():
        cot = jnp.concatenate([arrived[0][...], arrived[1][:HALF, :]], axis=0)
        below = cot.astype(f32) + conv_back(dpre[...].astype(f32), w)
        grads[...] = below.astype(bf16)
        head_out[...] = arrived[1][HALF:, :128].astype(f32)[:12]


def stack_kernel(*refs):
    near, far, out, scratch = refs[:4], refs[4:8], refs[9], refs[10]
    r = col_iota((48, 128))
    ph, pw = (r >> 3) & 3, r & 7
    for g in range(8):
        held = near[g][0:48, :] if g < 4 else far[g - 4][48:96, :]
        v = held.astype(f32)
        for tap in range(9):
            dh, dw = tap // 3 - 1, tap % 3 - 1
            shift = (-(8 * dh + dw)) % 128
            moved = pltpu.roll(v, shift, 1) if shift else v
            inside = (ph + dh >= 0) & (ph + dh < 4) & (pw + dw >= 0) & (pw + dw < 8)
            moved = jnp.where(inside, moved, 0.0)
            scratch[48 * tap : 48 * tap + 48, 128 * g : 128 * g + 128] = moved.astype(bf16)
    m = row_iota((448, 1))
    j = (m * 37450) >> 22
    rest = m - 112 * j
    i = (rest * 7282) >> 16
    source = jnp.where(rest < 108, (rest - 9 * i) * 48 + j * 12 + i, -1)
    pick = jnp.where(col_iota((448, 432)) == source, 1.0, 0.0).astype(bf16)
    out[...] = mm(pick, scratch[...]).astype(bf16)


def wgrad_kernel(stack, *refs):
    grads, outs = refs[:8], refs[8:]
    rows = jnp.concatenate([g[...] for g in grads], axis=0)
    total = mm(stack[...], rows)
    outs[0][...] = total[:112]
    outs[1][...] = total[112:336].astype(bf16)
    outs[2][...] = total[336:].astype(bf16)


def sum_kernel(own, pair, crossed, diagonal, out):
    total = own[...] + pair[:112, :].astype(f32)
    total = total + crossed[112:, :].astype(f32)
    total = total + diagonal[...].astype(f32)
    out[...] = total[:108].reshape(108, 1, CH)


def call(kernel, ins, outs, scratch=(), aliases=None):
    run = pl.pallas_call(
        kernel,
        out_shape=outs,
        in_specs=[pl.BlockSpec(memory_space=space) for space in ins],
        out_specs=jax.tree.map(
            lambda _: pl.BlockSpec(memory_space=VMEM), outs, is_leaf=lambda o: not isinstance(o, tuple)
        ),
        scratch_shapes=list(scratch),
        input_output_aliases=aliases or {},
        compiler_params=pltpu.CompilerParams(vmem_limit_bytes=24 << 20),
    )

    def with_operands(*operands):
        return run(
            *[
                value
                if space is SMEM
                else pltpu.with_memory_space_constraint(value, space)
                for value, space in zip(operands, ins, strict=True)
            ]
        )

    return with_operands


def sds(shape, dtype):
    return jax.ShapeDtypeStruct(shape, dtype)


def per_device(saved, kernels, head, counts, pairs, valid):
    ranks = lax.axis_size("dp")
    act = VMEM((ROWS, CH), bf16)
    msg_a, msg_b = VMEM((HALF, CH), bf16), VMEM((HALF + 16, CH), bf16)
    half_act = VMEM((HALF, CH), bf16)
    piece = VMEM((96, 128), bf16)
    gather = (0, 2, 8, 10)

    def swap(value, bits, odd_bits=None):
        pairs_of = [(d, d ^ (odd_bits if odd_bits and d & 1 else bits)) for d in range(ranks)]
        return lax.ppermute(value, "dp", pairs_of)

    def relayed(value, pairs_of):
        both = [(a, b) for a, b in pairs_of] + [(b, a) for a, b in pairs_of]
        return lax.ppermute(value, "section", both)

    slope, announce, rows, w, head = call(
        forward_kernel,
        [HBM] * 3 + [SMEM] + [HBM] * 2,
        (
            VMEM((ROWS, CH), f32),
            VMEM((256, 256), bf16),
            act,
            VMEM((3, 3, CH, CH), bf16),
            VMEM((CH, EMB), bf16),
        ),
        [SMEM((4,), jnp.int32), SMEM((4,), jnp.int32), pltpu.SemaphoreType.DMA((7,))],
    )(
        saved.reshape(ROWS, CH),
        jnp.transpose(kernels[0], (1, 2, 0, 3)),
        head,
        counts,
        pairs,
        valid,
    )
    gathered = lax.all_to_all(announce.reshape(32, 8, 256), "dp", 0, 0, tiled=True)
    sent_a, dpre3, head3, top = call(
        top_a_kernel, [VMEM] * 4, (msg_a, act, VMEM((16, EMB), f32), VMEM((8, CH), f32))
    )(gathered.reshape(256, 256), head, slope, w)
    arrived_a = relayed(sent_a, [(3, 2), (1, 0)])
    sent_b = call(top_b_kernel, [VMEM] * 4, msg_b)(top, dpre3, head3, w)
    arrived_b = relayed(sent_b, [(3, 2), (1, 0)])
    split = call(split_kernel, [VMEM] * 2, (piece,) * 4)(rows, sent_b)
    near = [split[0]] + [swap(split[k], gather[k]) for k in range(1, 4)]
    sent, held = [sent_a, sent_b], []

    def relay(active, half, arrived):
        message, dpre = call(
            functools.partial(relay_kernel, active, half),
            [VMEM] * 3,
            (msg_b if half else msg_a, half_act),
        )(arrived, slope, w)
        sent.append(message)
        held.append(dpre)
        return message

    for active, pairs_of in ((2, [(2, 1), (3, 0)]), (1, [(1, 0), (3, 2)])):
        next_a = relayed(relay(active, 0, arrived_a), pairs_of)
        next_b = relayed(relay(active, 1, arrived_b), pairs_of)
        arrived_a, arrived_b = next_a, next_b
    dpre = call(bottom_kernel, [VMEM] * 8, act)(
        arrived_a, arrived_b, slope, dpre3, *held
    )
    far = [swap(value, 1) for value in near]
    near_grads = [dpre] + [swap(dpre, gather[k]) for k in range(1, 4)]
    stack = call(
        stack_kernel, [VMEM] * 9, VMEM((448, 1024), bf16), [VMEM((432, 1024), bf16)]
    )(*near, *far, dpre)
    far_grads = [swap(value, 1) for value in near_grads]
    own, pair, diagonal = call(
        wgrad_kernel,
        [VMEM] * 9,
        (VMEM((112, CH), f32), VMEM((224, CH), bf16), VMEM((112, CH), bf16)),
    )(stack, *near_grads, *far_grads)
    pair = swap(pair, 6, 24)
    diagonal = swap(diagonal, 30)
    crossed = swap(pair, 1)
    grads, head_grad = call(
        last_kernel, [VMEM] * 12, (sds((ROWS, CH), bf16), sds((12, 128), f32))
    )(arrived_a, arrived_b, dpre, w, head3, *sent, own)
    wgrad = call(sum_kernel, [VMEM] * 4, sds((108, 1, CH), f32))(own, pair, crossed, diagonal)
    return (
        grads.reshape(saved.shape),
        wgrad.reshape(1, 12, 3, 3, CH),
        head_grad,
    )


def solution(mesh):
    return jax.shard_map(
        per_device,
        mesh=mesh,
        in_specs=(
            P("section", "dp", None, None, None),
            P("section", None, None, None, None),
            P(),
            P("dp"),
            P("dp"),
            P("dp"),
        ),
        out_specs=(
            P("section", "dp", None, None, None),
            P("section", "dp", None, None, None),
            P("dp", "section"),
        ),
        check_vma=False,
    )
```

```python
import jax
import jax.numpy as jnp
from jax import lax
from jax.experimental import pallas as pl
from jax.experimental.pallas import tpu as pltpu
from jax.sharding import PartitionSpec as P


tau_value = 0.2
loss_scale = 32.0
norm_eps = 1e-06
VMEM = pltpu.VMEM
SMEM = pltpu.SMEM
HBM = pltpu.HBM
f32 = jnp.float32
bf16 = jnp.bfloat16
NN = (((1,), (0,)), ((), ()))
NT = (((1,), (1,)), ((), ()))

ROWS, CELLS, CH, EMB = 128, 32, 384, 512


def mm(a, b, dims=NN):
    return lax.dot_general(a, b, dims, preferred_element_type=f32)


def row_iota(shape):
    return lax.broadcasted_iota(jnp.int32, shape, 0)


def col_iota(shape):
    return lax.broadcasted_iota(jnp.int32, shape, 1)


def position():
    rank = lax.axis_index("dp")
    return lax.axis_index("section"), rank, (rank >> 3), ((rank >> 1) & 3), (rank & 1)


def column_shifts(v):
    pw = row_iota((ROWS, 1)) & 7
    left = jnp.where(pw > 0, pltpu.roll(v, 1, 0), 0.0)
    right = jnp.where(pw < 7, pltpu.roll(v, ROWS - 1, 0), 0.0)
    return left, v, right


def row_shift(v, dh):
    if dh == 0:
        return v
    v = v.reshape(4, CELLS, CH)
    zero = jnp.zeros((4, 8, CH), v.dtype)
    if dh > 0:
        v = jnp.concatenate([v[:, 8:], zero], axis=1)
    else:
        v = jnp.concatenate([zero, v[:, :24]], axis=1)
    return v.reshape(ROWS, CH)


def conv_back(dpre, w):
    cols = column_shifts(dpre)
    lhs = [row_shift(cols[2 - tap % 3], 1 - tap // 3).astype(bf16) for tap in range(9)]
    rhs = [w[tap] for tap in range(9)]
    return mm(jnp.concatenate(lhs, axis=1), jnp.concatenate(rhs, axis=1), NT)


def forward_kernel(
    saved_hbm, w_hbm, head_hbm, counts, pairs_hbm, valid_hbm,
    slope, message, saved, w, head, pairs, valid, sem,
):
    sources = [saved_hbm] + [w_hbm.at[tap] for tap in range(9)]
    targets = [saved] + [w.at[tap] for tap in range(9)]
    sources += [pairs_hbm, valid_hbm, head_hbm]
    targets += [pairs, valid, head]
    copies = [
        pltpu.make_async_copy(source, target, sem.at[n])
        for n, (source, target) in enumerate(zip(sources, targets, strict=True))
    ]
    for copy in copies:
        copy.start()
    copies[0].wait()
    v = saved[...].astype(f32)
    cols = column_shifts(v)
    pre = None
    for taps in ((0, 1), (2, 3), (4, 5), (6, 7), (8,)):
        lhs = [row_shift(cols[tap % 3], tap // 3 - 1).astype(bf16) for tap in taps]
        for tap in taps:
            copies[1 + tap].wait()
        rhs = [w[tap] for tap in taps]
        part = mm(jnp.concatenate(lhs, axis=1), jnp.concatenate(rhs, axis=0))
        pre = part if pre is None else pre + part
    sigma = jax.nn.sigmoid(pre)
    slope[...] = sigma * (1.0 + pre * (1.0 - sigma))
    feature = (v + pre * sigma).reshape(4, CELLS, CH)
    pooled = jnp.sum(feature, axis=1) / CELLS
    for copy in copies[10:]:
        copy.wait()
    at = (row_iota((4, 128)), col_iota((4, 128)))
    extra = jnp.zeros((4, 128), f32)
    for slot in range(4):
        alive = jnp.logical_and(slot < counts[0], valid[slot] == 1)
        here = at[0] == slot
        extra = jnp.where(
            jnp.logical_and(here, at[1] == 0), jnp.where(alive, 1.0, 0.0).astype(f32), extra
        )
        extra = jnp.where(
            jnp.logical_and(here, at[1] == 1), pairs[slot].astype(f32), extra
        )
    packed = jnp.concatenate(
        [pooled[:, :256], jnp.concatenate([pooled[:, 256:], extra], axis=1)], axis=0
    )
    pair = jnp.concatenate([packed, packed], axis=0).astype(bf16)
    for at_row in range(0, 256, 16):
        message[at_row : at_row + 16, :] = pair


def contrast(gathered, head, rank):
    slot = row_iota((128, 256))
    lane = col_iota((128, 256))
    home = ((slot >> 2) << 3) + (slot & 3)
    first = mm(jnp.where(lane == home, 1.0, 0.0).astype(bf16), gathered)
    second = mm(jnp.where(lane == home + 4, 1.0, 0.0).astype(bf16), gathered)
    pooled = jnp.concatenate([first, second[:, :128]], axis=1).astype(bf16)
    live = second[:, 128:129]
    pairs = second[:, 129:130]
    proj = mm(pooled, head)
    inv = lax.rsqrt(jnp.sum(proj * proj, axis=1, keepdims=True) + norm_eps)
    unit = proj * inv
    unit_b = unit.astype(bf16)
    i = row_iota((128, 128))
    j = col_iota((128, 128))
    same = i == j

    def across(column):
        return jnp.sum(jnp.where(same, column, 0.0), axis=0, keepdims=True)

    expo = jnp.where(same, 0.0, jnp.exp(mm(unit_b, unit_b, NT) / tau_value))
    mate = pairs == j.astype(f32)
    live_row = across(live)
    total = jnp.sum(expo * live_row, axis=1, keepdims=True)
    share = live * jnp.sum(jnp.where(mate, live_row, 0.0), axis=1, keepdims=True)
    coef = (share / total).astype(bf16).astype(f32)
    coef_row = across(coef)
    mixing = expo * (coef * live_row + coef_row * live) - 2.0 * jnp.where(mate, share, 0.0)
    dunit = mm(mixing.astype(bf16), unit_b) * (loss_scale / tau_value)
    along = jnp.sum(unit * dunit, axis=1, keepdims=True)
    dproj = ((dunit - unit * along) * inv).astype(bf16)
    own = jnp.where(
        col_iota((16, 128)) == row_iota((16, 128)) + 4 * rank, 1.0, 0.0
    ).astype(bf16)
    dproj_own = mm(own, dproj).astype(bf16)
    dpooled = mm(dproj_own, head, NT).astype(bf16)
    mine = jnp.where(
        col_iota((16, CH)) == row_iota((16, CH)) + 12 * rank, 1.0, 0.0
    ).astype(bf16)
    pooled_mine = mm(mine, pooled, NT).astype(bf16)
    return dpooled[:4].astype(f32), mm(pooled_mine, dproj)


def split_kernel(saved, order, *outs):
    _, _, y, x, c = position()
    m = row_iota((CH, 1))
    q = (m * 43691) >> 19
    i = m - 12 * q
    j, k = q & 3, q >> 3
    core = c ^ ((q >> 2) & 1)
    flip_x = jnp.where((j == 3) | ((j > 0) & (core == 0)), 3, 0)
    flip_y = jnp.where((j == 3) | ((j > 0) & (core == 1)), 3, 0)
    to_y = y ^ (k >> 1) ^ flip_y
    to_x = x ^ (k & 1) ^ flip_x
    to_core = core ^ jnp.where(j == 2, 1, 0)
    channel = to_y * 96 + to_x * 24 + to_core * 12 + i
    pick = jnp.where(col_iota((CH, CH)) == channel, 1.0, 0.0).astype(bf16)
    turned = mm(pick, saved[...], NT).astype(bf16)
    for k, out in enumerate(outs):
        out[...] = turned[96 * k : 96 * k + 96]


def top_kernel(gathered, head, slope, w, message, dpre_out, head_out, head_sent):
    section, rank, _, _, _ = position()

    @pl.when(section == 3)
    def _():
        dpooled, head_grad = contrast(gathered[...], head[...], rank)
        top = (dpooled / CELLS).astype(bf16).astype(f32)
        cot = jnp.broadcast_to(top[:, None, :], (4, CELLS, CH)).reshape(ROWS, CH)
        dpre = (cot * slope[...]).astype(bf16)
        dpre_out[...] = dpre
        head_out[...] = head_grad[:, 384:]
        head_sent[...] = head_grad[:, :384].astype(bf16)
        below = cot + conv_back(dpre.astype(f32), w)
        message[...] = below.astype(bf16)


def relay(active, arrived, slope, w, message, dpre_out):
    @pl.when(lax.axis_index("section") == active)
    def _():
        cot = arrived[...].astype(f32)
        dpre = (cot * slope[...]).astype(bf16)
        dpre_out[...] = dpre
        below = cot + conv_back(dpre.astype(f32), w)
        message[...] = below.astype(bf16)


def relay2_kernel(arrived, slope, w, message, dpre_out):
    relay(2, arrived, slope, w, message, dpre_out)


def relay1_kernel(arrived, slope, w, message, dpre_out):
    relay(1, arrived, slope, w, message, dpre_out)


def bottom_kernel(arrived, slope, dpre3, dpre2, dpre1, *refs):
    section = lax.axis_index("section")
    dpre_out = refs[-1]
    for at, held in ((3, dpre3), (2, dpre2), (1, dpre1)):

        @pl.when(section == at)
        def _():
            dpre_out[...] = held[...]

    @pl.when(section == 0)
    def _():
        dpre_out[...] = (arrived[...].astype(f32) * slope[...]).astype(bf16)


def last_kernel(
    arrived, dpre, w, head3, head2, head1, head0, msg3, msg2, msg1, own, grads, head_out
):
    section = lax.axis_index("section")

    @pl.when(section == 3)
    def _():
        grads[...] = msg3[...]
        head_out[...] = head3[:12, :]

    for at, sent, head in ((2, msg2, head2), (1, msg1, head1)):

        @pl.when(section == at)
        def _():
            grads[...] = sent[...]
            head_out[...] = head[:, at * 128 : at * 128 + 128].astype(f32)[:12]

    @pl.when(section == 0)
    def _():
        below = arrived[...].astype(f32) + conv_back(dpre[...].astype(f32), w)
        grads[...] = below.astype(bf16)
        head_out[...] = head0[:, :128].astype(f32)[:12]


def stack_kernel(*refs):
    near, far, out, scratch = refs[:4], refs[4:8], refs[9], refs[10]
    r = col_iota((48, 128))
    ph, pw = (r >> 3) & 3, r & 7
    for g in range(8):
        held = far[g // 2][48:96, :] if g % 2 else near[g // 2][0:48, :]
        v = held.astype(f32)
        for tap in range(9):
            dh, dw = tap // 3 - 1, tap % 3 - 1
            shift = (-(8 * dh + dw)) % 128
            moved = pltpu.roll(v, shift, 1) if shift else v
            inside = (ph + dh >= 0) & (ph + dh < 4) & (pw + dw >= 0) & (pw + dw < 8)
            moved = jnp.where(inside, moved, 0.0)
            scratch[48 * tap : 48 * tap + 48, 128 * g : 128 * g + 128] = moved.astype(bf16)
    m = row_iota((448, 1))
    j = (m * 37450) >> 22
    rest = m - 112 * j
    i = (rest * 7282) >> 16
    source = jnp.where(rest < 108, (rest - 9 * i) * 48 + j * 12 + i, -1)
    pick = jnp.where(col_iota((448, 432)) == source, 1.0, 0.0).astype(bf16)
    out[...] = mm(pick, scratch[...]).astype(bf16)


def wgrad_a_kernel(stack, *refs):
    rows = jnp.concatenate([grad[...] for grad in refs[:6]], axis=0)
    refs[7][...] = mm(stack[:, :768], rows)


def wgrad_b_kernel(stack, part, near, far, own, pair, diagonal):
    rows = jnp.concatenate([near[...], far[...]], axis=0)
    total = part[...] + mm(stack[:, 768:], rows)
    own[...] = total[:112]
    pair[...] = total[112:336].astype(bf16)
    diagonal[...] = total[336:].astype(bf16)


def sum_kernel(own, pair, crossed, diagonal, out):
    total = own[...] + pair[:112, :].astype(f32)
    total = total + crossed[112:, :].astype(f32)
    total = total + diagonal[...].astype(f32)
    out[...] = total[:108].reshape(108, 1, CH)


def call(kernel, ins, outs, scratch=(), aliases=None):
    run = pl.pallas_call(
        kernel,
        out_shape=outs,
        in_specs=[pl.BlockSpec(memory_space=space) for space in ins],
        out_specs=jax.tree.map(
            lambda _: pl.BlockSpec(memory_space=VMEM), outs, is_leaf=lambda o: not isinstance(o, tuple)
        ),
        scratch_shapes=list(scratch),
        input_output_aliases=aliases or {},
        compiler_params=pltpu.CompilerParams(vmem_limit_bytes=24 << 20),
    )

    def with_operands(*operands):
        return run(
            *[
                value
                if space is SMEM
                else pltpu.with_memory_space_constraint(value, space)
                for value, space in zip(operands, ins, strict=True)
            ]
        )

    return with_operands


def sds(shape, dtype):
    return jax.ShapeDtypeStruct(shape, dtype)


def per_device(saved, kernels, head, counts, pairs, valid):
    ranks = lax.axis_size("dp")
    act = VMEM((ROWS, CH), bf16)
    piece = VMEM((96, 128), bf16)
    gather = (0, 2, 8, 10)

    def swap(value, bits, odd_bits=None):
        pairs_of = [(d, d ^ (odd_bits if odd_bits and d & 1 else bits)) for d in range(ranks)]
        return lax.ppermute(value, "dp", pairs_of)

    def relayed(value, pairs_of):
        both = [(a, b) for a, b in pairs_of] + [(b, a) for a, b in pairs_of]
        return lax.ppermute(value, "section", both)

    slope, announce, rows, w, head = call(
        forward_kernel,
        [HBM] * 3 + [SMEM] + [HBM] * 2,
        (
            VMEM((ROWS, CH), f32),
            VMEM((256, 256), bf16),
            act,
            VMEM((9, CH, CH), bf16),
            VMEM((CH, EMB), bf16),
        ),
        [SMEM((4,), jnp.int32), SMEM((4,), jnp.int32), pltpu.SemaphoreType.DMA((13,))],
    )(
        saved.reshape(ROWS, CH),
        jnp.transpose(kernels[0], (1, 2, 0, 3)).reshape(9, CH, CH),
        head,
        counts,
        pairs,
        valid,
    )
    gathered = lax.all_to_all(announce.reshape(32, 8, 256), "dp", 0, 0, tiled=True)
    msg3, dpre3, head3, head_sent = call(
        top_kernel, [VMEM] * 4, (act, act, VMEM((16, 128), f32), VMEM((16, CH), bf16))
    )(gathered.reshape(256, 256), head, slope, w)
    arrived = relayed(msg3, [(3, 2), (1, 0)])
    head2 = relayed(head_sent, [(3, 2), (1, 0)])
    split = call(split_kernel, [VMEM] * 2, (piece,) * 4)(rows, msg3)
    near = [split[0]] + [swap(split[k], gather[k]) for k in range(1, 4)]
    msg2, dpre2 = call(relay2_kernel, [VMEM] * 3, (act, act))(arrived, slope, w)
    arrived = relayed(msg2, [(2, 1), (3, 0)])
    head1 = relayed(head2, [(2, 1), (3, 0)])
    msg1, dpre1 = call(relay1_kernel, [VMEM] * 3, (act, act))(arrived, slope, w)
    arrived = relayed(msg1, [(1, 0), (3, 2)])
    head0 = relayed(head1, [(1, 0), (3, 2)])
    far = [swap(value, 1) for value in near]
    dpre = call(bottom_kernel, [VMEM] * 9, act)(
        arrived, slope, dpre3, dpre2, dpre1, *far
    )
    near_grads = [dpre] + [swap(dpre, gather[k]) for k in range(1, 4)]
    stack = call(
        stack_kernel, [VMEM] * 9, VMEM((448, 1024), bf16), [VMEM((432, 1024), bf16)]
    )(*near, *far, dpre)
    far_grads = [swap(value, 1) for value in near_grads]
    by_member = [value for both in zip(near_grads, far_grads) for value in both]
    part = call(wgrad_a_kernel, [VMEM] * 8, VMEM((448, CH), f32))(
        stack, *by_member[:6], near_grads[3]
    )
    own, pair, diagonal = call(
        wgrad_b_kernel,
        [VMEM] * 4,
        (VMEM((112, CH), f32), VMEM((224, CH), bf16), VMEM((112, CH), bf16)),
    )(stack, part, *by_member[6:])
    pair = swap(pair, 6, 24)
    diagonal = swap(diagonal, 30)
    crossed = swap(pair, 1)
    grads, head_grad = call(
        last_kernel, [VMEM] * 11, (sds((ROWS, CH), bf16), sds((12, 128), f32))
    )(arrived, dpre, w, head3, head2, head1, head0, msg3, msg2, msg1, own)
    wgrad = call(sum_kernel, [VMEM] * 4, sds((108, 1, CH), f32))(own, pair, crossed, diagonal)
    return (
        grads.reshape(saved.shape),
        wgrad.reshape(1, 12, 3, 3, CH),
        head_grad,
    )


def solution(mesh):
    return jax.shard_map(
        per_device,
        mesh=mesh,
        in_specs=(
            P("section", "dp", None, None, None),
            P("section", None, None, None, None),
            P(),
            P("dp"),
            P("dp"),
            P("dp"),
        ),
        out_specs=(
            P("section", "dp", None, None, None),
            P("section", "dp", None, None, None),
            P("dp", "section"),
        ),
        check_vma=False,
    )
```

```python
import jax
import jax.numpy as jnp
from jax import lax
from jax.experimental import pallas as pl
from jax.experimental.pallas import tpu as pltpu
from jax.sharding import PartitionSpec as P


tau_value = 0.2
loss_scale = 32.0
norm_eps = 1e-06
VMEM = pltpu.VMEM
SMEM = pltpu.SMEM
HBM = pltpu.HBM
f32 = jnp.float32
bf16 = jnp.bfloat16
NN = (((1,), (0,)), ((), ()))
NT = (((1,), (1,)), ((), ()))

ROWS, CELLS, CH, EMB = 128, 32, 384, 512


def mm(a, b, dims=NN):
    return lax.dot_general(a, b, dims, preferred_element_type=f32)


def row_iota(shape):
    return lax.broadcasted_iota(jnp.int32, shape, 0)


def col_iota(shape):
    return lax.broadcasted_iota(jnp.int32, shape, 1)


def position():
    rank = lax.axis_index("dp")
    return lax.axis_index("section"), rank, (rank >> 3), ((rank >> 1) & 3), (rank & 1)


def column_shifts(v):
    pw = row_iota((ROWS, 1)) & 7
    left = jnp.where(pw > 0, pltpu.roll(v, 1, 0), 0.0)
    right = jnp.where(pw < 7, pltpu.roll(v, ROWS - 1, 0), 0.0)
    return left, v, right


def row_shift(v, dh):
    if dh == 0:
        return v
    v = v.reshape(4, CELLS, CH)
    zero = jnp.zeros((4, 8, CH), v.dtype)
    if dh > 0:
        v = jnp.concatenate([v[:, 8:], zero], axis=1)
    else:
        v = jnp.concatenate([zero, v[:, :24]], axis=1)
    return v.reshape(ROWS, CH)


def conv_back(dpre, w):
    cols = column_shifts(dpre)
    total = None
    for kh in range(3):
        lhs = jnp.concatenate(
            [row_shift(cols[2 - kw], 1 - kh).astype(bf16) for kw in range(3)], axis=1
        )
        rhs = jnp.concatenate([w[kh, kw] for kw in range(3)], axis=1)
        part = mm(lhs, rhs, NT)
        total = part if total is None else total + part
    return total


def forward_kernel(
    saved_hbm, w_hbm, head_hbm, counts, pairs_hbm, valid_hbm,
    slope, message, saved, w, head, pairs, valid, sem,
):
    sources = [saved_hbm, w_hbm.at[0], w_hbm.at[1], w_hbm.at[2], pairs_hbm, valid_hbm, head_hbm]
    targets = [saved, w.at[0], w.at[1], w.at[2], pairs, valid, head]
    copies = [
        pltpu.make_async_copy(source, target, sem.at[n])
        for n, (source, target) in enumerate(zip(sources, targets, strict=True))
    ]
    for copy in copies:
        copy.start()
    copies[0].wait()
    v = saved[...].astype(f32)
    cols = column_shifts(v)
    pre = None
    for kh in range(3):
        lhs = jnp.concatenate(
            [row_shift(cols[kw], kh - 1).astype(bf16) for kw in range(3)], axis=1
        )
        copies[1 + kh].wait()
        part = mm(lhs, w[kh].reshape(3 * CH, CH))
        pre = part if pre is None else pre + part
    sigma = jax.nn.sigmoid(pre)
    slope[...] = sigma * (1.0 + pre * (1.0 - sigma))
    feature = (v + pre * sigma).reshape(4, CELLS, CH)
    pooled = jnp.sum(feature, axis=1) / CELLS
    for copy in copies[4:]:
        copy.wait()
    at = (row_iota((4, 128)), col_iota((4, 128)))
    extra = jnp.zeros((4, 128), f32)
    for slot in range(4):
        alive = jnp.logical_and(slot < counts[0], valid[slot] == 1)
        here = at[0] == slot
        extra = jnp.where(
            jnp.logical_and(here, at[1] == 0), jnp.where(alive, 1.0, 0.0).astype(f32), extra
        )
        extra = jnp.where(
            jnp.logical_and(here, at[1] == 1), pairs[slot].astype(f32), extra
        )
    packed = jnp.concatenate(
        [pooled[:, :256], jnp.concatenate([pooled[:, 256:], extra], axis=1)], axis=0
    )
    pair = jnp.concatenate([packed, packed], axis=0).astype(bf16)
    for at_row in range(0, 256, 16):
        message[at_row : at_row + 16, :] = pair


def scores_of(unit_b, others, ids, lanes):
    return jnp.where(ids == lanes, 0.0, jnp.exp(mm(unit_b, others, NT) / tau_value))


def normalized(pooled, head):
    proj = mm(pooled, head)
    inv = lax.rsqrt(jnp.sum(proj * proj, axis=1, keepdims=True) + norm_eps)
    return proj * inv, inv


def projected_grad(mixing, unit_b, unit, inv):
    dunit = mm(mixing, unit_b) * (loss_scale / tau_value)
    along = jnp.sum(unit * dunit, axis=1, keepdims=True)
    return ((dunit - unit * along) * inv).astype(bf16)


def slot_rows(gathered, home):
    lane = col_iota((home.shape[0], 256))
    first = mm(jnp.where(lane == home, 1.0, 0.0).astype(bf16), gathered)
    second = mm(jnp.where(lane == home + 4, 1.0, 0.0).astype(bf16), gathered)
    pooled = jnp.concatenate([first, second[:, :128]], axis=1).astype(bf16)
    return pooled, second[:, 128:129], second[:, 129:130]


def contrast(gathered, head, rank):
    slot = row_iota((128, 1))
    pooled, live, pairs = slot_rows(gathered, ((slot >> 2) << 3) + (slot & 3))
    own_slot = row_iota((16, 1))
    own_pooled, own_live, own_pairs = slot_rows(
        gathered, jnp.where(own_slot < 4, 8 * rank + own_slot, -8)
    )
    unit, inv = normalized(pooled, head)
    own_unit, own_inv = normalized(own_pooled, head)
    unit_b = unit.astype(bf16)
    j = col_iota((128, 128))
    same = slot == j

    def across(column):
        return jnp.sum(jnp.where(same, column, 0.0), axis=0, keepdims=True)

    live_row = across(live)

    def weights(expo, live, pairs):
        mate = pairs == col_iota(expo.shape).astype(f32)
        total = jnp.sum(expo * live_row, axis=1, keepdims=True)
        share = live * jnp.sum(jnp.where(mate, live_row, 0.0), axis=1, keepdims=True)
        coef = (share / total).astype(bf16).astype(f32)
        return coef, 2.0 * jnp.where(mate, share, 0.0)

    expo = scores_of(unit_b, unit_b, slot, j)
    own_expo = scores_of(own_unit.astype(bf16), unit_b, own_slot + 4 * rank, col_iota((16, 128)))
    coef, drawn = weights(expo, live, pairs)
    own_coef, own_drawn = weights(own_expo, own_live, own_pairs)
    coef_row = across(coef)
    mixing = expo * (coef * live_row + coef_row * live) - drawn
    own_mixing = own_expo * (own_coef * live_row + coef_row * own_live) - own_drawn
    dproj = projected_grad(own_mixing.astype(bf16), unit_b, own_unit, own_inv)
    dpooled = mm(dproj, head, NT).astype(bf16)
    mine = jnp.where(
        col_iota((16, CH)) == row_iota((16, CH)) + 12 * rank, 1.0, 0.0
    ).astype(bf16)
    pooled_mine = mm(mine, pooled, NT).astype(bf16)
    return dpooled[:4].astype(f32), (mixing.astype(bf16), unit, inv, pooled_mine)


def split_kernel(saved, order, *outs):
    _, _, y, x, c = position()
    m = row_iota((CH, 1))
    q = (m * 43691) >> 19
    i = m - 12 * q
    j, k = q & 3, q >> 3
    core = c ^ ((q >> 2) & 1)
    flip_x = jnp.where((j == 3) | ((j > 0) & (core == 0)), 3, 0)
    flip_y = jnp.where((j == 3) | ((j > 0) & (core == 1)), 3, 0)
    to_y = y ^ (k >> 1) ^ flip_y
    to_x = x ^ (k & 1) ^ flip_x
    to_core = core ^ jnp.where(j == 2, 1, 0)
    channel = to_y * 96 + to_x * 24 + to_core * 12 + i
    pick = jnp.where(col_iota((CH, CH)) == channel, 1.0, 0.0).astype(bf16)
    turned = mm(pick, saved[...], NT).astype(bf16)
    for k, out in enumerate(outs):
        out[...] = turned[96 * k : 96 * k + 96]


def top_kernel(
    gathered, head, slope, w, message, dpre_out, mixing_out, unit_out, inv_out, mine_out
):
    section, rank, _, _, _ = position()

    @pl.when(section == 3)
    def _():
        dpooled, (mixing, unit, inv, mine) = contrast(gathered[...], head[...], rank)
        mixing_out[...] = mixing
        unit_out[...] = unit
        inv_out[...] = jnp.broadcast_to(inv, (128, 128))
        mine_out[...] = mine
        top = (dpooled / CELLS).astype(bf16).astype(f32)
        cot = jnp.broadcast_to(top[:, None, :], (4, CELLS, CH)).reshape(ROWS, CH)
        dpre = (cot * slope[...]).astype(bf16)
        dpre_out[...] = dpre
        below = cot + conv_back(dpre.astype(f32), w)
        message[...] = below.astype(bf16)


def relay(active, arrived, slope, w, message, dpre_out):
    @pl.when(lax.axis_index("section") == active)
    def _():
        cot = arrived[...].astype(f32)
        dpre = (cot * slope[...]).astype(bf16)
        dpre_out[...] = dpre
        below = cot + conv_back(dpre.astype(f32), w)
        message[...] = below.astype(bf16)


def relay2_kernel(arrived, slope, w, mixing, unit, inv, mine, message, dpre_out, head_out):
    relay(2, arrived, slope, w, message, dpre_out)

    @pl.when(lax.axis_index("section") == 3)
    def _():
        units = unit[...]
        dproj = projected_grad(mixing[...], units.astype(bf16), units, inv[:, :1])
        head_grad = mm(mine[...], dproj)
        head_out[...] = head_grad
        message[:16, :] = head_grad[:, :384].astype(bf16)


def relay1_kernel(arrived, slope, w, head_grad, message, dpre_out):
    relay(1, arrived, slope, w, message, dpre_out)
    section = lax.axis_index("section")

    @pl.when(section == 3)
    def _():
        message[:16, :] = head_grad[:, :384].astype(bf16)

    @pl.when(section == 0)
    def _():
        message[:16, :] = arrived[:16, :]


def bottom_kernel(arrived, slope, dpre3, dpre2, dpre1, *refs):
    section = lax.axis_index("section")
    dpre_out = refs[-1]
    for at, held in ((3, dpre3), (2, dpre2), (1, dpre1)):

        @pl.when(section == at)
        def _():
            dpre_out[...] = held[...]

    @pl.when(section == 0)
    def _():
        dpre_out[...] = (arrived[...].astype(f32) * slope[...]).astype(bf16)


def last_kernel(arrived, earlier, dpre, w, head_grad, msg3, msg2, msg1, own, grads, head_out):
    section = lax.axis_index("section")

    @pl.when(section == 3)
    def _():
        grads[...] = msg3[...]
        head_out[...] = head_grad[:12, 384:]

    for at, sent in ((2, msg2), (1, msg1)):

        @pl.when(section == at)
        def _():
            grads[...] = sent[...]
            head_out[...] = arrived[:16, at * 128 : at * 128 + 128].astype(f32)[:12]

    @pl.when(section == 0)
    def _():
        below = arrived[...].astype(f32) + conv_back(dpre[...].astype(f32), w)
        grads[...] = below.astype(bf16)
        head_out[...] = earlier[:16, :128].astype(f32)[:12]


def stack_kernel(*refs):
    near, far, out, scratch = refs[:4], refs[4:8], refs[9], refs[10]
    r = col_iota((48, 128))
    ph, pw = (r >> 3) & 3, r & 7
    for g in range(8):
        held = near[g][0:48, :] if g < 4 else far[g - 4][48:96, :]
        v = held.astype(f32)
        for tap in range(9):
            dh, dw = tap // 3 - 1, tap % 3 - 1
            shift = (-(8 * dh + dw)) % 128
            moved = pltpu.roll(v, shift, 1) if shift else v
            inside = (ph + dh >= 0) & (ph + dh < 4) & (pw + dw >= 0) & (pw + dw < 8)
            moved = jnp.where(inside, moved, 0.0)
            scratch[48 * tap : 48 * tap + 48, 128 * g : 128 * g + 128] = moved.astype(bf16)
    m = row_iota((448, 1))
    j = (m * 37450) >> 22
    rest = m - 112 * j
    i = (rest * 7282) >> 16
    source = jnp.where(rest < 108, (rest - 9 * i) * 48 + j * 12 + i, -1)
    pick = jnp.where(col_iota((448, 432)) == source, 1.0, 0.0).astype(bf16)
    out[...] = mm(pick, scratch[...]).astype(bf16)


def wgrad_kernel(stack, *refs):
    grads, outs = refs[:8], refs[8:]
    rows = jnp.concatenate([g[...] for g in grads], axis=0)
    total = mm(stack[...], rows)
    outs[0][...] = total[:112]
    outs[1][...] = total[112:336].astype(bf16)
    outs[2][...] = total[336:].astype(bf16)


def sum_kernel(own, pair, crossed, diagonal, out):
    total = own[...] + pair[:112, :].astype(f32)
    total = total + crossed[112:, :].astype(f32)
    total = total + diagonal[...].astype(f32)
    out[...] = total[:108].reshape(108, 1, CH)


def call(kernel, ins, outs, scratch=(), aliases=None):
    run = pl.pallas_call(
        kernel,
        out_shape=outs,
        in_specs=[pl.BlockSpec(memory_space=space) for space in ins],
        out_specs=jax.tree.map(
            lambda _: pl.BlockSpec(memory_space=VMEM), outs, is_leaf=lambda o: not isinstance(o, tuple)
        ),
        scratch_shapes=list(scratch),
        input_output_aliases=aliases or {},
        compiler_params=pltpu.CompilerParams(vmem_limit_bytes=24 << 20),
    )

    def with_operands(*operands):
        return run(
            *[
                value
                if space is SMEM
                else pltpu.with_memory_space_constraint(value, space)
                for value, space in zip(operands, ins, strict=True)
            ]
        )

    return with_operands


def sds(shape, dtype):
    return jax.ShapeDtypeStruct(shape, dtype)


def per_device(saved, kernels, head, counts, pairs, valid):
    ranks = lax.axis_size("dp")
    act = VMEM((ROWS, CH), bf16)
    piece = VMEM((96, 128), bf16)
    gather = (0, 2, 8, 10)

    def swap(value, bits, odd_bits=None):
        pairs_of = [(d, d ^ (odd_bits if odd_bits and d & 1 else bits)) for d in range(ranks)]
        return lax.ppermute(value, "dp", pairs_of)

    def relayed(value, pairs_of):
        both = [(a, b) for a, b in pairs_of] + [(b, a) for a, b in pairs_of]
        return lax.ppermute(value, "section", both)

    slope, announce, rows, w, head = call(
        forward_kernel,
        [HBM] * 3 + [SMEM] + [HBM] * 2,
        (
            VMEM((ROWS, CH), f32),
            VMEM((256, 256), bf16),
            act,
            VMEM((3, 3, CH, CH), bf16),
            VMEM((CH, EMB), bf16),
        ),
        [SMEM((4,), jnp.int32), SMEM((4,), jnp.int32), pltpu.SemaphoreType.DMA((7,))],
    )(
        saved.reshape(ROWS, CH),
        jnp.transpose(kernels[0], (1, 2, 0, 3)),
        head,
        counts,
        pairs,
        valid,
    )
    gathered = lax.all_to_all(announce.reshape(32, 8, 256), "dp", 0, 0, tiled=True)
    msg3, dpre3, *for_head = call(
        top_kernel,
        [VMEM] * 4,
        (act, act, VMEM((128, 128), bf16), VMEM((128, EMB), f32), VMEM((128, 128), f32))
        + (VMEM((16, 128), bf16),),
    )(gathered.reshape(256, 256), head, slope, w)
    arrived = relayed(msg3, [(3, 2), (1, 0)])
    split = call(split_kernel, [VMEM] * 2, (piece,) * 4)(rows, msg3)
    near = [split[0]] + [swap(split[k], gather[k]) for k in range(1, 4)]
    msg2, dpre2, head_grad = call(
        relay2_kernel, [VMEM] * 7, (act, act, VMEM((16, EMB), f32))
    )(arrived, slope, w, *for_head)
    arrived = earlier = relayed(msg2, [(2, 1), (3, 0)])
    msg1, dpre1 = call(relay1_kernel, [VMEM] * 4, (act, act))(arrived, slope, w, head_grad)
    arrived = relayed(msg1, [(1, 0), (3, 2)])
    far = [swap(value, 1) for value in near]
    dpre = call(bottom_kernel, [VMEM] * 9, act)(
        arrived, slope, dpre3, dpre2, dpre1, *far
    )
    near_grads = [dpre] + [swap(dpre, gather[k]) for k in range(1, 4)]
    stack = call(
        stack_kernel, [VMEM] * 9, VMEM((448, 1024), bf16), [VMEM((432, 1024), bf16)]
    )(*near, *far, dpre)
    far_grads = [swap(value, 1) for value in near_grads]
    own, pair, diagonal = call(
        wgrad_kernel,
        [VMEM] * 9,
        (VMEM((112, CH), f32), VMEM((224, CH), bf16), VMEM((112, CH), bf16)),
    )(stack, *near_grads, *far_grads)
    pair = swap(pair, 6, 24)
    diagonal = swap(diagonal, 30)
    crossed = swap(pair, 1)
    grads, head_grad = call(
        last_kernel, [VMEM] * 9, (sds((ROWS, CH), bf16), sds((12, 128), f32))
    )(arrived, earlier, dpre, w, head_grad, msg3, msg2, msg1, own)
    wgrad = call(sum_kernel, [VMEM] * 4, sds((108, 1, CH), f32))(own, pair, crossed, diagonal)
    return (
        grads.reshape(saved.shape),
        wgrad.reshape(1, 12, 3, 3, CH),
        head_grad,
    )


def solution(mesh):
    return jax.shard_map(
        per_device,
        mesh=mesh,
        in_specs=(
            P("section", "dp", None, None, None),
            P("section", None, None, None, None),
            P(),
            P("dp"),
            P("dp"),
            P("dp"),
        ),
        out_specs=(
            P("section", "dp", None, None, None),
            P("section", "dp", None, None, None),
            P("dp", "section"),
        ),
        check_vma=False,
    )
```

```python
import jax
import jax.numpy as jnp
from jax import lax
from jax.experimental import pallas as pl
from jax.experimental.pallas import tpu as pltpu
from jax.sharding import PartitionSpec as P


tau_value = 0.2
loss_scale = 32.0
norm_eps = 1e-06
VMEM = pltpu.VMEM
SMEM = pltpu.SMEM
HBM = pltpu.HBM
f32 = jnp.float32
bf16 = jnp.bfloat16
NN = (((1,), (0,)), ((), ()))
NT = (((1,), (1,)), ((), ()))

ROWS, CELLS, CH, EMB = 128, 32, 384, 512


def mm(a, b, dims=NN):
    return lax.dot_general(a, b, dims, preferred_element_type=f32)


def row_iota(shape):
    return lax.broadcasted_iota(jnp.int32, shape, 0)


def col_iota(shape):
    return lax.broadcasted_iota(jnp.int32, shape, 1)


def position():
    rank = lax.axis_index("dp")
    return lax.axis_index("section"), rank, (rank >> 3), ((rank >> 1) & 3), (rank & 1)


def column_shifts(v):
    pw = row_iota((ROWS, 1)) & 7
    left = jnp.where(pw > 0, pltpu.roll(v, 1, 0), 0.0)
    right = jnp.where(pw < 7, pltpu.roll(v, ROWS - 1, 0), 0.0)
    return left, v, right


def row_shift(v, dh):
    if dh == 0:
        return v
    v = v.reshape(4, CELLS, CH)
    zero = jnp.zeros((4, 8, CH), v.dtype)
    if dh > 0:
        v = jnp.concatenate([v[:, 8:], zero], axis=1)
    else:
        v = jnp.concatenate([zero, v[:, :24]], axis=1)
    return v.reshape(ROWS, CH)


def conv_back(dpre, w):
    cols = column_shifts(dpre)
    total = None
    for kh in range(3):
        lhs = jnp.concatenate(
            [row_shift(cols[2 - kw], 1 - kh).astype(bf16) for kw in range(3)], axis=1
        )
        rhs = jnp.concatenate([w[kh, kw] for kw in range(3)], axis=1)
        part = mm(lhs, rhs, NT)
        total = part if total is None else total + part
    return total


def forward_kernel(
    saved_hbm, w_hbm, head_hbm, counts, pairs_hbm, valid_hbm,
    slope, message, saved, w, head, pairs, valid, sem,
):
    sources = [saved_hbm, w_hbm.at[0], w_hbm.at[1], w_hbm.at[2], pairs_hbm, valid_hbm, head_hbm]
    targets = [saved, w.at[0], w.at[1], w.at[2], pairs, valid, head]
    copies = [
        pltpu.make_async_copy(source, target, sem.at[n])
        for n, (source, target) in enumerate(zip(sources, targets, strict=True))
    ]
    for copy in copies:
        copy.start()
    copies[0].wait()
    v = saved[...].astype(f32)
    cols = column_shifts(v)
    pre = None
    for kh in range(3):
        lhs = jnp.concatenate(
            [row_shift(cols[kw], kh - 1).astype(bf16) for kw in range(3)], axis=1
        )
        copies[1 + kh].wait()
        part = mm(lhs, w[kh].reshape(3 * CH, CH))
        pre = part if pre is None else pre + part
    sigma = jax.nn.sigmoid(pre)
    slope[...] = sigma * (1.0 + pre * (1.0 - sigma))
    feature = (v + pre * sigma).reshape(4, CELLS, CH)
    pooled = jnp.sum(feature, axis=1) / CELLS
    for copy in copies[4:]:
        copy.wait()
    at = (row_iota((4, 128)), col_iota((4, 128)))
    extra = jnp.zeros((4, 128), f32)
    for slot in range(4):
        alive = jnp.logical_and(slot < counts[0], valid[slot] == 1)
        here = at[0] == slot
        extra = jnp.where(
            jnp.logical_and(here, at[1] == 0), jnp.where(alive, 1.0, 0.0).astype(f32), extra
        )
        extra = jnp.where(
            jnp.logical_and(here, at[1] == 1), pairs[slot].astype(f32), extra
        )
    packed = jnp.concatenate(
        [pooled[:, :256], jnp.concatenate([pooled[:, 256:], extra], axis=1)], axis=0
    )
    pair = jnp.concatenate([packed, packed], axis=0).astype(bf16)
    for at_row in range(0, 256, 16):
        message[at_row : at_row + 16, :] = pair


def scores_of(unit_b, others, ids, lanes):
    return jnp.where(ids == lanes, 0.0, jnp.exp(mm(unit_b, others, NT) / tau_value))


def normalized(pooled, head):
    proj = mm(pooled, head)
    inv = lax.rsqrt(jnp.sum(proj * proj, axis=1, keepdims=True) + norm_eps)
    return proj * inv, inv


def projected_grad(mixing, unit_b, unit, inv):
    dunit = mm(mixing, unit_b) * (loss_scale / tau_value)
    along = jnp.sum(unit * dunit, axis=1, keepdims=True)
    return ((dunit - unit * along) * inv).astype(bf16)


def slot_rows(gathered, home):
    lane = col_iota((home.shape[0], 256))
    first = mm(jnp.where(lane == home, 1.0, 0.0).astype(bf16), gathered)
    second = mm(jnp.where(lane == home + 4, 1.0, 0.0).astype(bf16), gathered)
    pooled = jnp.concatenate([first, second[:, :128]], axis=1).astype(bf16)
    return pooled, second[:, 128:129], second[:, 129:130]


def contrast(gathered, head, rank):
    slot = row_iota((128, 1))
    pooled, live, pairs = slot_rows(gathered, ((slot >> 2) << 3) + (slot & 3))
    own_slot = row_iota((16, 1))
    own_pooled, own_live, own_pairs = slot_rows(
        gathered, jnp.where(own_slot < 4, 8 * rank + own_slot, -8)
    )
    unit, inv = normalized(pooled, head)
    own_unit, own_inv = normalized(own_pooled, head)
    unit_b = unit.astype(bf16)
    j = col_iota((128, 128))
    same = slot == j

    def across(column):
        return jnp.sum(jnp.where(same, column, 0.0), axis=0, keepdims=True)

    live_row = across(live)

    def weights(expo, live, pairs):
        mate = pairs == col_iota(expo.shape).astype(f32)
        total = jnp.sum(expo * live_row, axis=1, keepdims=True)
        share = live * jnp.sum(jnp.where(mate, live_row, 0.0), axis=1, keepdims=True)
        coef = (share / total).astype(bf16).astype(f32)
        return coef, 2.0 * jnp.where(mate, share, 0.0)

    expo = scores_of(unit_b, unit_b, slot, j)
    own_expo = scores_of(own_unit.astype(bf16), unit_b, own_slot + 4 * rank, col_iota((16, 128)))
    coef, drawn = weights(expo, live, pairs)
    own_coef, own_drawn = weights(own_expo, own_live, own_pairs)
    coef_row = across(coef)
    mixing = expo * (coef * live_row + coef_row * live) - drawn
    own_mixing = own_expo * (own_coef * live_row + coef_row * own_live) - own_drawn
    dproj = projected_grad(own_mixing.astype(bf16), unit_b, own_unit, own_inv)
    dpooled = mm(dproj, head, NT).astype(bf16)
    mine = jnp.where(
        col_iota((16, CH)) == row_iota((16, CH)) + 12 * rank, 1.0, 0.0
    ).astype(bf16)
    pooled_mine = mm(mine, pooled, NT).astype(bf16)
    return dpooled[:4].astype(f32), (mixing.astype(bf16), unit, inv, pooled_mine)


def split_kernel(saved, order, *outs):
    _, _, y, x, c = position()
    m = row_iota((CH, 1))
    q = (m * 43691) >> 19
    i = m - 12 * q
    j, k = q & 3, q >> 3
    core = c ^ ((q >> 2) & 1)
    flip_x = jnp.where((j == 3) | ((j > 0) & (core == 0)), 3, 0)
    flip_y = jnp.where((j == 3) | ((j > 0) & (core == 1)), 3, 0)
    to_y = y ^ (k >> 1) ^ flip_y
    to_x = x ^ (k & 1) ^ flip_x
    to_core = core ^ jnp.where(j == 2, 1, 0)
    channel = to_y * 96 + to_x * 24 + to_core * 12 + i
    pick = jnp.where(col_iota((CH, CH)) == channel, 1.0, 0.0).astype(bf16)
    turned = mm(pick, saved[...], NT).astype(bf16)
    for k, out in enumerate(outs):
        out[...] = turned[96 * k : 96 * k + 96]


def top_kernel(
    gathered, head, slope, w, message, dpre_out, mixing_out, unit_out, inv_out, mine_out
):
    section, rank, _, _, _ = position()

    @pl.when(section == 3)
    def _():
        dpooled, (mixing, unit, inv, mine) = contrast(gathered[...], head[...], rank)
        mixing_out[...] = mixing
        unit_out[...] = unit
        inv_out[...] = jnp.broadcast_to(inv, (128, 128))
        mine_out[...] = mine
        top = (dpooled / CELLS).astype(bf16).astype(f32)
        cot = jnp.broadcast_to(top[:, None, :], (4, CELLS, CH)).reshape(ROWS, CH)
        dpre = (cot * slope[...]).astype(bf16)
        dpre_out[...] = dpre
        below = cot + conv_back(dpre.astype(f32), w)
        message[...] = below.astype(bf16)


def relay(active, arrived, slope, w, message, dpre_out):
    @pl.when(lax.axis_index("section") == active)
    def _():
        cot = arrived[...].astype(f32)
        dpre = (cot * slope[...]).astype(bf16)
        dpre_out[...] = dpre
        below = cot + conv_back(dpre.astype(f32), w)
        message[...] = below.astype(bf16)


def relay2_kernel(
    arrived, slope, w, mixing, unit, inv, mine, message, dpre_out, head_out, head_sent
):
    relay(2, arrived, slope, w, message, dpre_out)

    @pl.when(lax.axis_index("section") == 3)
    def _():
        units = unit[...]
        dproj = projected_grad(mixing[...], units.astype(bf16), units, inv[:, :1])
        head_grad = mm(mine[...], dproj)
        head_out[...] = head_grad[:, 384:]
        head_sent[...] = head_grad[:, :128].astype(bf16)
        message[:16, :] = head_grad[:, :384].astype(bf16)


def relay1_kernel(arrived, slope, w, message, dpre_out):
    relay(1, arrived, slope, w, message, dpre_out)

    @pl.when(lax.axis_index("section") == 2)
    def _():
        message[:16, :] = arrived[:16, :]


def bottom_kernel(arrived, slope, dpre3, dpre2, dpre1, *refs):
    section = lax.axis_index("section")
    dpre_out = refs[-1]
    for at, held in ((3, dpre3), (2, dpre2), (1, dpre1)):

        @pl.when(section == at)
        def _():
            dpre_out[...] = held[...]

    @pl.when(section == 0)
    def _():
        dpre_out[...] = (arrived[...].astype(f32) * slope[...]).astype(bf16)


def last_kernel(
    arrived, earlier, head_up, dpre, w, head_grad, msg3, msg2, msg1, own, grads, head_out
):
    section = lax.axis_index("section")

    @pl.when(section == 3)
    def _():
        grads[...] = msg3[...]
        head_out[...] = head_grad[:12, :]

    for at, sent, head in ((2, msg2, earlier), (1, msg1, arrived)):

        @pl.when(section == at)
        def _():
            grads[...] = sent[...]
            head_out[...] = head[:16, at * 128 : at * 128 + 128].astype(f32)[:12]

    @pl.when(section == 0)
    def _():
        below = arrived[...].astype(f32) + conv_back(dpre[...].astype(f32), w)
        grads[...] = below.astype(bf16)
        head_out[...] = head_up[...].astype(f32)[:12]


def stack_kernel(*refs):
    near, far, out, scratch = refs[:4], refs[4:8], refs[9], refs[10]
    r = col_iota((48, 128))
    ph, pw = (r >> 3) & 3, r & 7
    for g in range(8):
        held = near[g][0:48, :] if g < 4 else far[g - 4][48:96, :]
        v = held.astype(f32)
        for tap in range(9):
            dh, dw = tap // 3 - 1, tap % 3 - 1
            shift = (-(8 * dh + dw)) % 128
            moved = pltpu.roll(v, shift, 1) if shift else v
            inside = (ph + dh >= 0) & (ph + dh < 4) & (pw + dw >= 0) & (pw + dw < 8)
            moved = jnp.where(inside, moved, 0.0)
            scratch[48 * tap : 48 * tap + 48, 128 * g : 128 * g + 128] = moved.astype(bf16)
    m = row_iota((448, 1))
    j = (m * 37450) >> 22
    rest = m - 112 * j
    i = (rest * 7282) >> 16
    source = jnp.where(rest < 108, (rest - 9 * i) * 48 + j * 12 + i, -1)
    pick = jnp.where(col_iota((448, 432)) == source, 1.0, 0.0).astype(bf16)
    out[...] = mm(pick, scratch[...]).astype(bf16)


def wgrad_kernel(stack, *refs):
    grads, outs = refs[:8], refs[8:]
    rows = jnp.concatenate([g[...] for g in grads], axis=0)
    total = mm(stack[...], rows)
    outs[0][...] = total[:112]
    outs[1][...] = total[112:336].astype(bf16)
    outs[2][...] = total[336:].astype(bf16)


def sum_kernel(own, pair, crossed, diagonal, out):
    total = own[...] + pair[:112, :].astype(f32)
    total = total + crossed[112:, :].astype(f32)
    total = total + diagonal[...].astype(f32)
    out[...] = total[:108].reshape(108, 1, CH)


def call(kernel, ins, outs, scratch=(), aliases=None):
    run = pl.pallas_call(
        kernel,
        out_shape=outs,
        in_specs=[pl.BlockSpec(memory_space=space) for space in ins],
        out_specs=jax.tree.map(
            lambda _: pl.BlockSpec(memory_space=VMEM), outs, is_leaf=lambda o: not isinstance(o, tuple)
        ),
        scratch_shapes=list(scratch),
        input_output_aliases=aliases or {},
        compiler_params=pltpu.CompilerParams(vmem_limit_bytes=24 << 20),
    )

    def with_operands(*operands):
        return run(
            *[
                value
                if space is SMEM
                else pltpu.with_memory_space_constraint(value, space)
                for value, space in zip(operands, ins, strict=True)
            ]
        )

    return with_operands


def sds(shape, dtype):
    return jax.ShapeDtypeStruct(shape, dtype)


def per_device(saved, kernels, head, counts, pairs, valid):
    ranks = lax.axis_size("dp")
    sections = lax.axis_size("section")
    act = VMEM((ROWS, CH), bf16)
    piece = VMEM((96, 128), bf16)
    gather = (0, 2, 8, 10)

    def swap(value, bits, odd_bits=None):
        pairs_of = [(d, d ^ (odd_bits if odd_bits and d & 1 else bits)) for d in range(ranks)]
        return lax.ppermute(value, "dp", pairs_of)

    def relayed(value, step=-1):
        around = [(at, (at + step) % sections) for at in range(sections)]
        return lax.ppermute(value, "section", around)

    slope, announce, rows, w, head = call(
        forward_kernel,
        [HBM] * 3 + [SMEM] + [HBM] * 2,
        (
            VMEM((ROWS, CH), f32),
            VMEM((256, 256), bf16),
            act,
            VMEM((3, 3, CH, CH), bf16),
            VMEM((CH, EMB), bf16),
        ),
        [SMEM((4,), jnp.int32), SMEM((4,), jnp.int32), pltpu.SemaphoreType.DMA((7,))],
    )(
        saved.reshape(ROWS, CH),
        jnp.transpose(kernels[0], (1, 2, 0, 3)),
        head,
        counts,
        pairs,
        valid,
    )
    gathered = lax.all_to_all(announce.reshape(32, 8, 256), "dp", 0, 0, tiled=True)
    msg3, dpre3, *for_head = call(
        top_kernel,
        [VMEM] * 4,
        (act, act, VMEM((128, 128), bf16), VMEM((128, EMB), f32), VMEM((128, 128), f32))
        + (VMEM((16, 128), bf16),),
    )(gathered.reshape(256, 256), head, slope, w)
    arrived = relayed(msg3)
    split = call(split_kernel, [VMEM] * 2, (piece,) * 4)(rows, msg3)
    near = [split[0]] + [swap(split[k], gather[k]) for k in range(1, 4)]
    msg2, dpre2, head_grad, head_sent = call(
        relay2_kernel, [VMEM] * 7, (act, act, VMEM((16, 128), f32), VMEM((16, 128), bf16))
    )(arrived, slope, w, *for_head)
    arrived = earlier = relayed(msg2)
    head_up = relayed(head_sent, 1)
    msg1, dpre1 = call(relay1_kernel, [VMEM] * 3, (act, act))(arrived, slope, w)
    arrived = relayed(msg1)
    far = [swap(value, 1) for value in near]
    dpre = call(bottom_kernel, [VMEM] * 9, act)(
        arrived, slope, dpre3, dpre2, dpre1, *far
    )
    near_grads = [dpre] + [swap(dpre, gather[k]) for k in range(1, 4)]
    stack = call(
        stack_kernel, [VMEM] * 9, VMEM((448, 1024), bf16), [VMEM((432, 1024), bf16)]
    )(*near, *far, dpre)
    far_grads = [swap(value, 1) for value in near_grads]
    own, pair, diagonal = call(
        wgrad_kernel,
        [VMEM] * 9,
        (VMEM((112, CH), f32), VMEM((224, CH), bf16), VMEM((112, CH), bf16)),
    )(stack, *near_grads, *far_grads)
    pair = swap(pair, 6, 24)
    diagonal = swap(diagonal, 30)
    crossed = swap(pair, 1)
    grads, head_grad = call(
        last_kernel, [VMEM] * 10, (sds((ROWS, CH), bf16), sds((12, 128), f32))
    )(arrived, earlier, head_up, dpre, w, head_grad, msg3, msg2, msg1, own)
    wgrad = call(sum_kernel, [VMEM] * 4, sds((108, 1, CH), f32))(own, pair, crossed, diagonal)
    return (
        grads.reshape(saved.shape),
        wgrad.reshape(1, 12, 3, 3, CH),
        head_grad,
    )


def solution(mesh):
    return jax.shard_map(
        per_device,
        mesh=mesh,
        in_specs=(
            P("section", "dp", None, None, None),
            P("section", None, None, None, None),
            P(),
            P("dp"),
            P("dp"),
            P("dp"),
        ),
        out_specs=(
            P("section", "dp", None, None, None),
            P("section", "dp", None, None, None),
            P("dp", "section"),
        ),
        check_vma=False,
    )
```

```python
import jax
import jax.numpy as jnp
from jax import lax
from jax.experimental import pallas as pl
from jax.experimental.pallas import tpu as pltpu
from jax.sharding import PartitionSpec as P


tau_value = 0.2
loss_scale = 32.0
norm_eps = 1e-06
VMEM = pltpu.VMEM
SMEM = pltpu.SMEM
HBM = pltpu.HBM
f32 = jnp.float32
bf16 = jnp.bfloat16
NN = (((1,), (0,)), ((), ()))
NT = (((1,), (1,)), ((), ()))

ROWS, CELLS, CH, EMB = 128, 32, 384, 512


def mm(a, b, dims=NN):
    return lax.dot_general(a, b, dims, preferred_element_type=f32)


def row_iota(shape):
    return lax.broadcasted_iota(jnp.int32, shape, 0)


def col_iota(shape):
    return lax.broadcasted_iota(jnp.int32, shape, 1)


def position():
    rank = lax.axis_index("dp")
    return lax.axis_index("section"), rank, (rank >> 3), ((rank >> 1) & 3), (rank & 1)


def column_shifts(v):
    pw = row_iota((ROWS, 1)) & 7
    left = jnp.where(pw > 0, pltpu.roll(v, 1, 0), 0.0)
    right = jnp.where(pw < 7, pltpu.roll(v, ROWS - 1, 0), 0.0)
    return left, v, right


def row_shift(v, dh):
    if dh == 0:
        return v
    v = v.reshape(4, CELLS, CH)
    zero = jnp.zeros((4, 8, CH), v.dtype)
    if dh > 0:
        v = jnp.concatenate([v[:, 8:], zero], axis=1)
    else:
        v = jnp.concatenate([zero, v[:, :24]], axis=1)
    return v.reshape(ROWS, CH)


def conv_back(dpre, w):
    cols = column_shifts(dpre)
    total = None
    for kh in range(3):
        lhs = jnp.concatenate(
            [row_shift(cols[2 - kw], 1 - kh).astype(bf16) for kw in range(3)], axis=1
        )
        rhs = jnp.concatenate([w[kh, kw] for kw in range(3)], axis=1)
        part = mm(lhs, rhs, NT)
        total = part if total is None else total + part
    return total


def forward_kernel(
    saved_hbm, w_hbm, head_hbm, counts, pairs_hbm, valid_hbm,
    slope, message, saved, w, head, pairs, valid, sem,
):
    sources = [saved_hbm, w_hbm.at[0], w_hbm.at[1], w_hbm.at[2], pairs_hbm, valid_hbm, head_hbm]
    targets = [saved, w.at[0], w.at[1], w.at[2], pairs, valid, head]
    copies = [
        pltpu.make_async_copy(source, target, sem.at[n])
        for n, (source, target) in enumerate(zip(sources, targets, strict=True))
    ]
    for copy in copies:
        copy.start()
    copies[0].wait()
    v = saved[...].astype(f32)
    cols = column_shifts(v)
    pre = None
    for kh in range(3):
        lhs = jnp.concatenate(
            [row_shift(cols[kw], kh - 1).astype(bf16) for kw in range(3)], axis=1
        )
        copies[1 + kh].wait()
        part = mm(lhs, w[kh].reshape(3 * CH, CH))
        pre = part if pre is None else pre + part
    sigma = jax.nn.sigmoid(pre)
    slope[...] = sigma * (1.0 + pre * (1.0 - sigma))
    feature = (v + pre * sigma).reshape(4, CELLS, CH)
    pooled = jnp.sum(feature, axis=1) / CELLS
    for copy in copies[4:]:
        copy.wait()
    at = (row_iota((4, 128)), col_iota((4, 128)))
    extra = jnp.zeros((4, 128), f32)
    for slot in range(4):
        alive = jnp.logical_and(slot < counts[0], valid[slot] == 1)
        here = at[0] == slot
        extra = jnp.where(
            jnp.logical_and(here, at[1] == 0), jnp.where(alive, 1.0, 0.0).astype(f32), extra
        )
        extra = jnp.where(
            jnp.logical_and(here, at[1] == 1), pairs[slot].astype(f32), extra
        )
    packed = jnp.concatenate(
        [pooled[:, :256], jnp.concatenate([pooled[:, 256:], extra], axis=1)], axis=0
    )
    pair = jnp.concatenate([packed, packed], axis=0).astype(bf16)
    for at_row in range(0, 256, 16):
        message[at_row : at_row + 16, :] = pair


def scores_of(unit_b, others, ids, lanes):
    return jnp.where(ids == lanes, 0.0, jnp.exp(mm(unit_b, others, NT) / tau_value))


def normalized(pooled, head):
    proj = mm(pooled, head)
    inv = lax.rsqrt(jnp.sum(proj * proj, axis=1, keepdims=True) + norm_eps)
    return proj * inv, inv


def projected_grad(mixing, unit_b, unit, inv):
    dunit = mm(mixing, unit_b) * (loss_scale / tau_value)
    along = jnp.sum(unit * dunit, axis=1, keepdims=True)
    return ((dunit - unit * along) * inv).astype(bf16)


def slot_rows(gathered, home):
    lane = col_iota((home.shape[0], 256))
    first = mm(jnp.where(lane == home, 1.0, 0.0).astype(bf16), gathered)
    second = mm(jnp.where(lane == home + 4, 1.0, 0.0).astype(bf16), gathered)
    pooled = jnp.concatenate([first, second[:, :128]], axis=1).astype(bf16)
    return pooled, second[:, 128:129], second[:, 129:130]


def contrast(gathered, head, rank):
    slot = row_iota((128, 1))
    pooled, live, pairs = slot_rows(gathered, ((slot >> 2) << 3) + (slot & 3))
    own_slot = row_iota((16, 1))
    own_pooled, own_live, own_pairs = slot_rows(
        gathered, jnp.where(own_slot < 4, 8 * rank + own_slot, -8)
    )
    unit, inv = normalized(pooled, head)
    own_unit, own_inv = normalized(own_pooled, head)
    unit_b = unit.astype(bf16)
    j = col_iota((128, 128))
    same = slot == j

    def across(column):
        return jnp.sum(jnp.where(same, column, 0.0), axis=0, keepdims=True)

    live_row = across(live)

    def weights(expo, live, pairs):
        mate = pairs == col_iota(expo.shape).astype(f32)
        total = jnp.sum(expo * live_row, axis=1, keepdims=True)
        share = live * jnp.sum(jnp.where(mate, live_row, 0.0), axis=1, keepdims=True)
        coef = (share / total).astype(bf16).astype(f32)
        return coef, 2.0 * jnp.where(mate, share, 0.0)

    expo = scores_of(unit_b, unit_b, slot, j)
    own_expo = scores_of(own_unit.astype(bf16), unit_b, own_slot + 4 * rank, col_iota((16, 128)))
    coef, drawn = weights(expo, live, pairs)
    own_coef, own_drawn = weights(own_expo, own_live, own_pairs)
    coef_row = across(coef)
    mixing = expo * (coef * live_row + coef_row * live) - drawn
    own_mixing = own_expo * (own_coef * live_row + coef_row * own_live) - own_drawn
    dproj = projected_grad(own_mixing.astype(bf16), unit_b, own_unit, own_inv)
    dpooled = mm(dproj, head, NT).astype(bf16)
    mine = jnp.where(
        col_iota((16, CH)) == row_iota((16, CH)) + 12 * rank, 1.0, 0.0
    ).astype(bf16)
    pooled_mine = mm(mine, pooled, NT).astype(bf16)
    return dpooled[:4].astype(f32), (mixing.astype(bf16), unit, inv, pooled_mine)


def split_kernel(saved, order, *outs):
    _, _, y, x, c = position()
    m = row_iota((CH, 1))
    q = (m * 43691) >> 19
    i = m - 12 * q
    j, k = q & 3, q >> 3
    core = c ^ ((q >> 2) & 1)
    flip_x = jnp.where((j == 3) | ((j > 0) & (core == 0)), 3, 0)
    flip_y = jnp.where((j == 3) | ((j > 0) & (core == 1)), 3, 0)
    to_y = y ^ (k >> 1) ^ flip_y
    to_x = x ^ (k & 1) ^ flip_x
    to_core = core ^ jnp.where(j == 2, 1, 0)
    channel = to_y * 96 + to_x * 24 + to_core * 12 + i
    pick = jnp.where(col_iota((CH, CH)) == channel, 1.0, 0.0).astype(bf16)
    turned = mm(pick, saved[...], NT).astype(bf16)
    for k, out in enumerate(outs):
        out[...] = turned[96 * k : 96 * k + 96]


def top_kernel(
    gathered, head, slope, w, message, dpre_out, mixing_out, unit_out, inv_out, mine_out
):
    section, rank, _, _, _ = position()

    @pl.when(section == 3)
    def _():
        dpooled, (mixing, unit, inv, mine) = contrast(gathered[...], head[...], rank)
        mixing_out[...] = mixing
        unit_out[...] = unit
        inv_out[...] = jnp.broadcast_to(inv, (128, 128))
        mine_out[...] = mine
        top = (dpooled / CELLS).astype(bf16).astype(f32)
        cot = jnp.broadcast_to(top[:, None, :], (4, CELLS, CH)).reshape(ROWS, CH)
        dpre = (cot * slope[...]).astype(bf16)
        dpre_out[...] = dpre
        below = cot + conv_back(dpre.astype(f32), w)
        message[...] = below.astype(bf16)


def relay(active, arrived, slope, w, message, dpre_out):
    @pl.when(lax.axis_index("section") == active)
    def _():
        cot = arrived[...].astype(f32)
        dpre = (cot * slope[...]).astype(bf16)
        dpre_out[...] = dpre
        below = cot + conv_back(dpre.astype(f32), w)
        message[...] = below.astype(bf16)


def relay2_kernel(arrived, slope, w, mixing, unit, inv, mine, message, dpre_out, head_out):
    relay(2, arrived, slope, w, message, dpre_out)

    @pl.when(lax.axis_index("section") == 3)
    def _():
        units = unit[...]
        dproj = projected_grad(mixing[...], units.astype(bf16), units, inv[:, :1])
        head_grad = mm(mine[...], dproj)
        head_out[...] = head_grad
        message[:16, :] = head_grad[:, :384].astype(bf16)


def relay1_kernel(arrived, slope, w, head_grad, message, dpre_out, head_sent):
    relay(1, arrived, slope, w, message, dpre_out)
    section = lax.axis_index("section")

    @pl.when(section == 3)
    def _():
        head_sent[...] = head_grad[:, :384].astype(bf16)

    @pl.when(section == 2)
    def _():
        head_sent[...] = arrived[:16, :]


def bottom_kernel(arrived, slope, dpre3, dpre2, dpre1, *refs):
    section = lax.axis_index("section")
    dpre_out = refs[-1]
    for at, held in ((3, dpre3), (2, dpre2), (1, dpre1)):

        @pl.when(section == at)
        def _():
            dpre_out[...] = held[...]

    @pl.when(section == 0)
    def _():
        dpre_out[...] = (arrived[...].astype(f32) * slope[...]).astype(bf16)


def last_kernel(
    arrived, earlier, head_down, dpre, w, head_grad, msg3, msg2, msg1, own, grads, head_out
):
    section = lax.axis_index("section")

    @pl.when(section == 3)
    def _():
        grads[...] = msg3[...]
        head_out[...] = head_grad[:12, 384:]

    for at, sent, head in ((2, msg2, earlier), (1, msg1, head_down)):

        @pl.when(section == at)
        def _():
            grads[...] = sent[...]
            head_out[...] = head[:16, at * 128 : at * 128 + 128].astype(f32)[:12]

    @pl.when(section == 0)
    def _():
        below = arrived[...].astype(f32) + conv_back(dpre[...].astype(f32), w)
        grads[...] = below.astype(bf16)
        head_out[...] = head_down[:, :128].astype(f32)[:12]


def stack_kernel(*refs):
    near, far, out, scratch = refs[:4], refs[4:8], refs[9], refs[10]
    r = col_iota((48, 128))
    ph, pw = (r >> 3) & 3, r & 7
    for g in range(8):
        held = near[g][0:48, :] if g < 4 else far[g - 4][48:96, :]
        v = held.astype(f32)
        for tap in range(9):
            dh, dw = tap // 3 - 1, tap % 3 - 1
            shift = (-(8 * dh + dw)) % 128
            moved = pltpu.roll(v, shift, 1) if shift else v
            inside = (ph + dh >= 0) & (ph + dh < 4) & (pw + dw >= 0) & (pw + dw < 8)
            moved = jnp.where(inside, moved, 0.0)
            scratch[48 * tap : 48 * tap + 48, 128 * g : 128 * g + 128] = moved.astype(bf16)
    m = row_iota((448, 1))
    j = (m * 37450) >> 22
    rest = m - 112 * j
    i = (rest * 7282) >> 16
    source = jnp.where(rest < 108, (rest - 9 * i) * 48 + j * 12 + i, -1)
    pick = jnp.where(col_iota((448, 432)) == source, 1.0, 0.0).astype(bf16)
    out[...] = mm(pick, scratch[...]).astype(bf16)


def wgrad_kernel(stack, *refs):
    grads, outs = refs[:8], refs[8:]
    rows = jnp.concatenate([g[...] for g in grads], axis=0)
    total = mm(stack[...], rows)
    outs[0][...] = total[:112]
    outs[1][...] = total[112:336].astype(bf16)
    outs[2][...] = total[336:].astype(bf16)


def sum_kernel(own, pair, crossed, diagonal, out):
    total = own[...] + pair[:112, :].astype(f32)
    total = total + crossed[112:, :].astype(f32)
    total = total + diagonal[...].astype(f32)
    out[...] = total[:108].reshape(108, 1, CH)


def call(kernel, ins, outs, scratch=(), aliases=None):
    run = pl.pallas_call(
        kernel,
        out_shape=outs,
        in_specs=[pl.BlockSpec(memory_space=space) for space in ins],
        out_specs=jax.tree.map(
            lambda _: pl.BlockSpec(memory_space=VMEM), outs, is_leaf=lambda o: not isinstance(o, tuple)
        ),
        scratch_shapes=list(scratch),
        input_output_aliases=aliases or {},
        compiler_params=pltpu.CompilerParams(vmem_limit_bytes=24 << 20),
    )

    def with_operands(*operands):
        return run(
            *[
                value
                if space is SMEM
                else pltpu.with_memory_space_constraint(value, space)
                for value, space in zip(operands, ins, strict=True)
            ]
        )

    return with_operands


def sds(shape, dtype):
    return jax.ShapeDtypeStruct(shape, dtype)


def per_device(saved, kernels, head, counts, pairs, valid):
    ranks = lax.axis_size("dp")
    act = VMEM((ROWS, CH), bf16)
    piece = VMEM((96, 128), bf16)
    gather = (0, 2, 8, 10)

    def swap(value, bits, odd_bits=None):
        pairs_of = [(d, d ^ (odd_bits if odd_bits and d & 1 else bits)) for d in range(ranks)]
        return lax.ppermute(value, "dp", pairs_of)

    def relayed(value, routes):
        return lax.ppermute(value, "section", routes)

    def swaps(*pairs_of):
        return [(a, b) for a, b in pairs_of] + [(b, a) for a, b in pairs_of]

    slope, announce, rows, w, head = call(
        forward_kernel,
        [HBM] * 3 + [SMEM] + [HBM] * 2,
        (
            VMEM((ROWS, CH), f32),
            VMEM((256, 256), bf16),
            act,
            VMEM((3, 3, CH, CH), bf16),
            VMEM((CH, EMB), bf16),
        ),
        [SMEM((4,), jnp.int32), SMEM((4,), jnp.int32), pltpu.SemaphoreType.DMA((7,))],
    )(
        saved.reshape(ROWS, CH),
        jnp.transpose(kernels[0], (1, 2, 0, 3)),
        head,
        counts,
        pairs,
        valid,
    )
    gathered = lax.all_to_all(announce.reshape(32, 8, 256), "dp", 0, 0, tiled=True)
    msg3, dpre3, *for_head = call(
        top_kernel,
        [VMEM] * 4,
        (act, act, VMEM((128, 128), bf16), VMEM((128, EMB), f32), VMEM((128, 128), f32))
        + (VMEM((16, 128), bf16),),
    )(gathered.reshape(256, 256), head, slope, w)
    arrived = relayed(msg3, swaps((3, 2), (1, 0)))
    split = call(split_kernel, [VMEM] * 2, (piece,) * 4)(rows, msg3)
    near = [split[0]] + [swap(split[k], gather[k]) for k in range(1, 4)]
    msg2, dpre2, head_grad = call(
        relay2_kernel, [VMEM] * 7, (act, act, VMEM((16, EMB), f32))
    )(arrived, slope, w, *for_head)
    arrived = earlier = relayed(msg2, [(3, 2), (2, 1), (1, 0), (0, 3)])
    msg1, dpre1, head_sent = call(
        relay1_kernel, [VMEM] * 4, (act, act, VMEM((16, CH), bf16))
    )(arrived, slope, w, head_grad)
    arrived = relayed(msg1, swaps((1, 0), (3, 2)))
    head_down = relayed(head_sent, swaps((3, 0), (2, 1)))
    far = [swap(value, 1) for value in near]
    dpre = call(bottom_kernel, [VMEM] * 9, act)(
        arrived, slope, dpre3, dpre2, dpre1, *far
    )
    near_grads = [dpre] + [swap(dpre, gather[k]) for k in range(1, 4)]
    stack = call(
        stack_kernel, [VMEM] * 9, VMEM((448, 1024), bf16), [VMEM((432, 1024), bf16)]
    )(*near, *far, dpre)
    far_grads = [swap(value, 1) for value in near_grads]
    own, pair, diagonal = call(
        wgrad_kernel,
        [VMEM] * 9,
        (VMEM((112, CH), f32), VMEM((224, CH), bf16), VMEM((112, CH), bf16)),
    )(stack, *near_grads, *far_grads)
    pair = swap(pair, 6, 24)
    diagonal = swap(diagonal, 30)
    crossed = swap(pair, 1)
    grads, head_grad = call(
        last_kernel, [VMEM] * 10, (sds((ROWS, CH), bf16), sds((12, 128), f32))
    )(arrived, earlier, head_down, dpre, w, head_grad, msg3, msg2, msg1, own)
    wgrad = call(sum_kernel, [VMEM] * 4, sds((108, 1, CH), f32))(own, pair, crossed, diagonal)
    return (
        grads.reshape(saved.shape),
        wgrad.reshape(1, 12, 3, 3, CH),
        head_grad,
    )


def solution(mesh):
    return jax.shard_map(
        per_device,
        mesh=mesh,
        in_specs=(
            P("section", "dp", None, None, None),
            P("section", None, None, None, None),
            P(),
            P("dp"),
            P("dp"),
            P("dp"),
        ),
        out_specs=(
            P("section", "dp", None, None, None),
            P("section", "dp", None, None, None),
            P("dp", "section"),
        ),
        check_vma=False,
    )
```

```python
import jax
import jax.numpy as jnp
from jax import lax
from jax.experimental import pallas as pl
from jax.experimental.pallas import tpu as pltpu
from jax.sharding import PartitionSpec as P


tau_value = 0.2
loss_scale = 32.0
norm_eps = 1e-06
VMEM = pltpu.VMEM
SMEM = pltpu.SMEM
HBM = pltpu.HBM
f32 = jnp.float32
bf16 = jnp.bfloat16
NN = (((1,), (0,)), ((), ()))
NT = (((1,), (1,)), ((), ()))

ROWS, CELLS, CH, EMB = 128, 32, 384, 512


def mm(a, b, dims=NN):
    return lax.dot_general(a, b, dims, preferred_element_type=f32)


def row_iota(shape):
    return lax.broadcasted_iota(jnp.int32, shape, 0)


def col_iota(shape):
    return lax.broadcasted_iota(jnp.int32, shape, 1)


def position():
    rank = lax.axis_index("dp")
    return lax.axis_index("section"), rank, (rank >> 3), ((rank >> 1) & 3), (rank & 1)


def column_shifts(v):
    pw = row_iota((ROWS, 1)) & 7
    left = jnp.where(pw > 0, pltpu.roll(v, 1, 0), 0.0)
    right = jnp.where(pw < 7, pltpu.roll(v, ROWS - 1, 0), 0.0)
    return left, v, right


def row_shift(v, dh):
    if dh == 0:
        return v
    v = v.reshape(4, CELLS, CH)
    zero = jnp.zeros((4, 8, CH), v.dtype)
    if dh > 0:
        v = jnp.concatenate([v[:, 8:], zero], axis=1)
    else:
        v = jnp.concatenate([zero, v[:, :24]], axis=1)
    return v.reshape(ROWS, CH)


def conv_back(dpre, w):
    cols = column_shifts(dpre)
    total = None
    for kh in range(3):
        lhs = jnp.concatenate(
            [row_shift(cols[2 - kw], 1 - kh).astype(bf16) for kw in range(3)], axis=1
        )
        rhs = jnp.concatenate([w[kh, kw] for kw in range(3)], axis=1)
        part = mm(lhs, rhs, NT)
        total = part if total is None else total + part
    return total


def forward_kernel(
    saved_hbm, w_hbm, head_hbm, counts, pairs_hbm, valid_hbm,
    slope, message, saved, w, head, pairs, valid, sem,
):
    sources = [saved_hbm, w_hbm.at[0], w_hbm.at[1], w_hbm.at[2], pairs_hbm, valid_hbm, head_hbm]
    targets = [saved, w.at[0], w.at[1], w.at[2], pairs, valid, head]
    copies = [
        pltpu.make_async_copy(source, target, sem.at[n])
        for n, (source, target) in enumerate(zip(sources, targets, strict=True))
    ]
    for copy in copies:
        copy.start()
    copies[0].wait()
    v = saved[...].astype(f32)
    cols = column_shifts(v)
    pre = None
    for kh in range(3):
        lhs = jnp.concatenate(
            [row_shift(cols[kw], kh - 1).astype(bf16) for kw in range(3)], axis=1
        )
        copies[1 + kh].wait()
        part = mm(lhs, w[kh].reshape(3 * CH, CH))
        pre = part if pre is None else pre + part
    sigma = jax.nn.sigmoid(pre)
    slope[...] = sigma * (1.0 + pre * (1.0 - sigma))
    feature = (v + pre * sigma).reshape(4, CELLS, CH)
    pooled = jnp.sum(feature, axis=1) / CELLS
    for copy in copies[4:]:
        copy.wait()
    at = (row_iota((4, 128)), col_iota((4, 128)))
    extra = jnp.zeros((4, 128), f32)
    for slot in range(4):
        alive = jnp.logical_and(slot < counts[0], valid[slot] == 1)
        here = at[0] == slot
        extra = jnp.where(
            jnp.logical_and(here, at[1] == 0), jnp.where(alive, 1.0, 0.0).astype(f32), extra
        )
        extra = jnp.where(
            jnp.logical_and(here, at[1] == 1), pairs[slot].astype(f32), extra
        )
    packed = jnp.concatenate(
        [pooled[:, :256], jnp.concatenate([pooled[:, 256:], extra], axis=1)], axis=0
    )
    pair = jnp.concatenate([packed, packed], axis=0).astype(bf16)
    for at_row in range(0, 256, 16):
        message[at_row : at_row + 16, :] = pair


def scores_of(unit_b, others, ids, lanes):
    return jnp.where(ids == lanes, 0.0, jnp.exp(mm(unit_b, others, NT) / tau_value))


def normalized(pooled, head):
    proj = mm(pooled, head)
    inv = lax.rsqrt(jnp.sum(proj * proj, axis=1, keepdims=True) + norm_eps)
    return proj * inv, inv


def projected_grad(mixing, unit_b, unit, inv):
    dunit = mm(mixing, unit_b) * (loss_scale / tau_value)
    along = jnp.sum(unit * dunit, axis=1, keepdims=True)
    return ((dunit - unit * along) * inv).astype(bf16)


def slot_rows(gathered, home):
    lane = col_iota((home.shape[0], 256))
    first = mm(jnp.where(lane == home, 1.0, 0.0).astype(bf16), gathered)
    second = mm(jnp.where(lane == home + 4, 1.0, 0.0).astype(bf16), gathered)
    pooled = jnp.concatenate([first, second[:, :128]], axis=1).astype(bf16)
    return pooled, second[:, 128:129], second[:, 129:130]


def contrast(gathered, head, rank):
    slot = row_iota((128, 1))
    pooled, live, pairs = slot_rows(gathered, ((slot >> 2) << 3) + (slot & 3))
    own_slot = row_iota((16, 1))
    own_pooled, own_live, own_pairs = slot_rows(
        gathered, jnp.where(own_slot < 4, 8 * rank + own_slot, -8)
    )
    unit, inv = normalized(pooled, head)
    own_unit, own_inv = normalized(own_pooled, head)
    unit_b = unit.astype(bf16)
    j = col_iota((128, 128))
    same = slot == j

    def across(column):
        return jnp.sum(jnp.where(same, column, 0.0), axis=0, keepdims=True)

    live_row = across(live)

    def weights(expo, live, pairs):
        mate = pairs == col_iota(expo.shape).astype(f32)
        total = jnp.sum(expo * live_row, axis=1, keepdims=True)
        share = live * jnp.sum(jnp.where(mate, live_row, 0.0), axis=1, keepdims=True)
        coef = (share / total).astype(bf16).astype(f32)
        return coef, 2.0 * jnp.where(mate, share, 0.0)

    expo = scores_of(unit_b, unit_b, slot, j)
    own_expo = scores_of(own_unit.astype(bf16), unit_b, own_slot + 4 * rank, col_iota((16, 128)))
    coef, drawn = weights(expo, live, pairs)
    own_coef, own_drawn = weights(own_expo, own_live, own_pairs)
    coef_row = across(coef)
    mixing = expo * (coef * live_row + coef_row * live) - drawn
    own_mixing = own_expo * (own_coef * live_row + coef_row * own_live) - own_drawn
    dproj = projected_grad(own_mixing.astype(bf16), unit_b, own_unit, own_inv)
    dpooled = mm(dproj, head, NT).astype(bf16)
    mine = jnp.where(
        col_iota((16, CH)) == row_iota((16, CH)) + 12 * rank, 1.0, 0.0
    ).astype(bf16)
    pooled_mine = mm(mine, pooled, NT).astype(bf16)
    return dpooled[:4].astype(f32), (mixing.astype(bf16), unit, inv, pooled_mine)


def split_kernel(saved, order, mixing, unit, inv, mine, head_out, *outs):
    _, _, y, x, c = position()
    m = row_iota((CH, 1))
    q = (m * 43691) >> 19
    i = m - 12 * q
    j, k = q & 3, q >> 3
    core = c ^ ((q >> 2) & 1)
    flip_x = jnp.where((j == 3) | ((j > 0) & (core == 0)), 3, 0)
    flip_y = jnp.where((j == 3) | ((j > 0) & (core == 1)), 3, 0)
    to_y = y ^ (k >> 1) ^ flip_y
    to_x = x ^ (k & 1) ^ flip_x
    to_core = core ^ jnp.where(j == 2, 1, 0)
    channel = to_y * 96 + to_x * 24 + to_core * 12 + i
    pick = jnp.where(col_iota((CH, CH)) == channel, 1.0, 0.0).astype(bf16)
    turned = mm(pick, saved[...], NT).astype(bf16)
    for k, out in enumerate(outs):
        out[...] = turned[96 * k : 96 * k + 96]

    @pl.when(lax.axis_index("section") == 3)
    def _():
        units = unit[...]
        dproj = projected_grad(mixing[...], units.astype(bf16), units, inv[:, :1])
        head_out[...] = mm(mine[...], dproj)


def top_kernel(
    gathered, head, slope, w, message, dpre_out, mixing_out, unit_out, inv_out, mine_out
):
    section, rank, _, _, _ = position()

    @pl.when(section == 3)
    def _():
        dpooled, (mixing, unit, inv, mine) = contrast(gathered[...], head[...], rank)
        mixing_out[...] = mixing
        unit_out[...] = unit
        inv_out[...] = jnp.broadcast_to(inv, (128, 128))
        mine_out[...] = mine
        top = (dpooled / CELLS).astype(bf16).astype(f32)
        cot = jnp.broadcast_to(top[:, None, :], (4, CELLS, CH)).reshape(ROWS, CH)
        dpre = (cot * slope[...]).astype(bf16)
        dpre_out[...] = dpre
        below = cot + conv_back(dpre.astype(f32), w)
        message[...] = below.astype(bf16)


def relay(active, arrived, slope, w, message, dpre_out):
    @pl.when(lax.axis_index("section") == active)
    def _():
        cot = arrived[...].astype(f32)
        dpre = (cot * slope[...]).astype(bf16)
        dpre_out[...] = dpre
        below = cot + conv_back(dpre.astype(f32), w)
        message[...] = below.astype(bf16)


def relay2_kernel(arrived, slope, w, head_grad, message, dpre_out):
    relay(2, arrived, slope, w, message, dpre_out)

    @pl.when(lax.axis_index("section") == 3)
    def _():
        message[:16, :] = head_grad[:, :384].astype(bf16)


def relay1_kernel(arrived, slope, w, head_grad, message, dpre_out):
    relay(1, arrived, slope, w, message, dpre_out)
    section = lax.axis_index("section")

    @pl.when(section == 3)
    def _():
        message[:16, :] = head_grad[:, :384].astype(bf16)

    @pl.when(section == 0)
    def _():
        message[:16, :] = arrived[:16, :]


def bottom_kernel(arrived, slope, dpre3, dpre2, dpre1, *refs):
    section = lax.axis_index("section")
    dpre_out = refs[-1]
    for at, held in ((3, dpre3), (2, dpre2), (1, dpre1)):

        @pl.when(section == at)
        def _():
            dpre_out[...] = held[...]

    @pl.when(section == 0)
    def _():
        dpre_out[...] = (arrived[...].astype(f32) * slope[...]).astype(bf16)


def last_kernel(arrived, earlier, dpre, w, head_grad, msg3, msg2, msg1, own, grads, head_out):
    section = lax.axis_index("section")

    @pl.when(section == 3)
    def _():
        grads[...] = msg3[...]
        head_out[...] = head_grad[:12, 384:]

    for at, sent in ((2, msg2), (1, msg1)):

        @pl.when(section == at)
        def _():
            grads[...] = sent[...]
            head_out[...] = arrived[:16, at * 128 : at * 128 + 128].astype(f32)[:12]

    @pl.when(section == 0)
    def _():
        below = arrived[...].astype(f32) + conv_back(dpre[...].astype(f32), w)
        grads[...] = below.astype(bf16)
        head_out[...] = earlier[:16, :128].astype(f32)[:12]


def stack_kernel(*refs):
    near, far, out, scratch = refs[:4], refs[4:8], refs[9], refs[10]
    r = col_iota((48, 128))
    ph, pw = (r >> 3) & 3, r & 7
    for g in range(8):
        held = near[g][0:48, :] if g < 4 else far[g - 4][48:96, :]
        v = held.astype(f32)
        for tap in range(9):
            dh, dw = tap // 3 - 1, tap % 3 - 1
            shift = (-(8 * dh + dw)) % 128
            moved = pltpu.roll(v, shift, 1) if shift else v
            inside = (ph + dh >= 0) & (ph + dh < 4) & (pw + dw >= 0) & (pw + dw < 8)
            moved = jnp.where(inside, moved, 0.0)
            scratch[48 * tap : 48 * tap + 48, 128 * g : 128 * g + 128] = moved.astype(bf16)
    m = row_iota((448, 1))
    j = (m * 37450) >> 22
    rest = m - 112 * j
    i = (rest * 7282) >> 16
    source = jnp.where(rest < 108, (rest - 9 * i) * 48 + j * 12 + i, -1)
    pick = jnp.where(col_iota((448, 432)) == source, 1.0, 0.0).astype(bf16)
    out[...] = mm(pick, scratch[...]).astype(bf16)


def wgrad_kernel(stack, *refs):
    grads, outs = refs[:8], refs[8:]
    rows = jnp.concatenate([g[...] for g in grads], axis=0)
    total = mm(stack[...], rows)
    outs[0][...] = total[:112]
    outs[1][...] = total[112:336].astype(bf16)
    outs[2][...] = total[336:].astype(bf16)


def sum_kernel(own, pair, crossed, diagonal, out):
    total = own[...] + pair[:112, :].astype(f32)
    total = total + crossed[112:, :].astype(f32)
    total = total + diagonal[...].astype(f32)
    out[...] = total[:108].reshape(108, 1, CH)


def call(kernel, ins, outs, scratch=(), aliases=None):
    run = pl.pallas_call(
        kernel,
        out_shape=outs,
        in_specs=[pl.BlockSpec(memory_space=space) for space in ins],
        out_specs=jax.tree.map(
            lambda _: pl.BlockSpec(memory_space=VMEM), outs, is_leaf=lambda o: not isinstance(o, tuple)
        ),
        scratch_shapes=list(scratch),
        input_output_aliases=aliases or {},
        compiler_params=pltpu.CompilerParams(vmem_limit_bytes=24 << 20),
    )

    def with_operands(*operands):
        return run(
            *[
                value
                if space is SMEM
                else pltpu.with_memory_space_constraint(value, space)
                for value, space in zip(operands, ins, strict=True)
            ]
        )

    return with_operands


def sds(shape, dtype):
    return jax.ShapeDtypeStruct(shape, dtype)


def per_device(saved, kernels, head, counts, pairs, valid):
    ranks = lax.axis_size("dp")
    act = VMEM((ROWS, CH), bf16)
    piece = VMEM((96, 128), bf16)
    gather = (0, 2, 8, 10)

    def swap(value, bits, odd_bits=None):
        pairs_of = [(d, d ^ (odd_bits if odd_bits and d & 1 else bits)) for d in range(ranks)]
        return lax.ppermute(value, "dp", pairs_of)

    def relayed(value, pairs_of):
        both = [(a, b) for a, b in pairs_of] + [(b, a) for a, b in pairs_of]
        return lax.ppermute(value, "section", both)

    slope, announce, rows, w, head = call(
        forward_kernel,
        [HBM] * 3 + [SMEM] + [HBM] * 2,
        (
            VMEM((ROWS, CH), f32),
            VMEM((256, 256), bf16),
            act,
            VMEM((3, 3, CH, CH), bf16),
            VMEM((CH, EMB), bf16),
        ),
        [SMEM((4,), jnp.int32), SMEM((4,), jnp.int32), pltpu.SemaphoreType.DMA((7,))],
    )(
        saved.reshape(ROWS, CH),
        jnp.transpose(kernels[0], (1, 2, 0, 3)),
        head,
        counts,
        pairs,
        valid,
    )
    gathered = lax.all_to_all(announce.reshape(32, 8, 256), "dp", 0, 0, tiled=True)
    msg3, dpre3, *for_head = call(
        top_kernel,
        [VMEM] * 4,
        (act, act, VMEM((128, 128), bf16), VMEM((128, EMB), f32), VMEM((128, 128), f32))
        + (VMEM((16, 128), bf16),),
    )(gathered.reshape(256, 256), head, slope, w)
    arrived = relayed(msg3, [(3, 2), (1, 0)])
    head_grad, *split = call(
        split_kernel, [VMEM] * 6, (VMEM((16, EMB), f32),) + (piece,) * 4
    )(rows, msg3, *for_head)
    near = [split[0]] + [swap(split[k], gather[k]) for k in range(1, 4)]
    msg2, dpre2 = call(relay2_kernel, [VMEM] * 4, (act, act))(arrived, slope, w, head_grad)
    arrived = earlier = relayed(msg2, [(2, 1), (3, 0)])
    msg1, dpre1 = call(relay1_kernel, [VMEM] * 4, (act, act))(arrived, slope, w, head_grad)
    arrived = relayed(msg1, [(1, 0), (3, 2)])
    far = [swap(value, 1) for value in near]
    dpre = call(bottom_kernel, [VMEM] * 9, act)(
        arrived, slope, dpre3, dpre2, dpre1, *far
    )
    near_grads = [dpre] + [swap(dpre, gather[k]) for k in range(1, 4)]
    stack = call(
        stack_kernel, [VMEM] * 9, VMEM((448, 1024), bf16), [VMEM((432, 1024), bf16)]
    )(*near, *far, dpre)
    far_grads = [swap(value, 1) for value in near_grads]
    own, pair, diagonal = call(
        wgrad_kernel,
        [VMEM] * 9,
        (VMEM((112, CH), f32), VMEM((224, CH), bf16), VMEM((112, CH), bf16)),
    )(stack, *near_grads, *far_grads)
    pair = swap(pair, 6, 24)
    diagonal = swap(diagonal, 30)
    crossed = swap(pair, 1)
    grads, head_grad = call(
        last_kernel, [VMEM] * 9, (sds((ROWS, CH), bf16), sds((12, 128), f32))
    )(arrived, earlier, dpre, w, head_grad, msg3, msg2, msg1, own)
    wgrad = call(sum_kernel, [VMEM] * 4, sds((108, 1, CH), f32))(own, pair, crossed, diagonal)
    return (
        grads.reshape(saved.shape),
        wgrad.reshape(1, 12, 3, 3, CH),
        head_grad,
    )


def solution(mesh):
    return jax.shard_map(
        per_device,
        mesh=mesh,
        in_specs=(
            P("section", "dp", None, None, None),
            P("section", None, None, None, None),
            P(),
            P("dp"),
            P("dp"),
            P("dp"),
        ),
        out_specs=(
            P("section", "dp", None, None, None),
            P("section", "dp", None, None, None),
            P("dp", "section"),
        ),
        check_vma=False,
    )
```

```python
import jax
import jax.numpy as jnp
from jax import lax
from jax.experimental import pallas as pl
from jax.experimental.pallas import tpu as pltpu
from jax.sharding import PartitionSpec as P


tau_value = 0.2
loss_scale = 32.0
norm_eps = 1e-06
VMEM = pltpu.VMEM
SMEM = pltpu.SMEM
HBM = pltpu.HBM
f32 = jnp.float32
bf16 = jnp.bfloat16
NN = (((1,), (0,)), ((), ()))
NT = (((1,), (1,)), ((), ()))

ROWS, CELLS, CH, EMB = 128, 32, 384, 512


def mm(a, b, dims=NN):
    return lax.dot_general(a, b, dims, preferred_element_type=f32)


def row_iota(shape):
    return lax.broadcasted_iota(jnp.int32, shape, 0)


def col_iota(shape):
    return lax.broadcasted_iota(jnp.int32, shape, 1)


def position():
    rank = lax.axis_index("dp")
    return lax.axis_index("section"), rank, (rank >> 3), ((rank >> 1) & 3), (rank & 1)


def column_shifts(v):
    pw = row_iota((ROWS, 1)) & 7
    left = jnp.where(pw > 0, pltpu.roll(v, 1, 0), 0.0)
    right = jnp.where(pw < 7, pltpu.roll(v, ROWS - 1, 0), 0.0)
    return left, v, right


def row_shift(v, dh):
    if dh == 0:
        return v
    v = v.reshape(4, CELLS, CH)
    zero = jnp.zeros((4, 8, CH), v.dtype)
    if dh > 0:
        v = jnp.concatenate([v[:, 8:], zero], axis=1)
    else:
        v = jnp.concatenate([zero, v[:, :24]], axis=1)
    return v.reshape(ROWS, CH)


def conv_back(dpre, w):
    cols = column_shifts(dpre)
    taps = [(kh, kw) for kh in range(3) for kw in range(3)]
    lhs = [row_shift(cols[2 - kw], 1 - kh).astype(bf16) for kh, kw in taps]
    rhs = [w[kh, kw] for kh, kw in taps]
    return mm(jnp.concatenate(lhs, axis=1), jnp.concatenate(rhs, axis=1), NT)


def forward_kernel(
    saved_hbm, w_hbm, head_hbm, counts, pairs_hbm, valid_hbm,
    slope, message, saved, w, head, pairs, valid, sem,
):
    sources = [saved_hbm, w_hbm.at[0], w_hbm.at[1], w_hbm.at[2], pairs_hbm, valid_hbm, head_hbm]
    targets = [saved, w.at[0], w.at[1], w.at[2], pairs, valid, head]
    copies = [
        pltpu.make_async_copy(source, target, sem.at[n])
        for n, (source, target) in enumerate(zip(sources, targets, strict=True))
    ]
    for copy in copies:
        copy.start()
    copies[0].wait()
    v = saved[...].astype(f32)
    cols = column_shifts(v)
    pre = None
    for kh in range(3):
        lhs = jnp.concatenate(
            [row_shift(cols[kw], kh - 1).astype(bf16) for kw in range(3)], axis=1
        )
        copies[1 + kh].wait()
        part = mm(lhs, w[kh].reshape(3 * CH, CH))
        pre = part if pre is None else pre + part
    sigma = jax.nn.sigmoid(pre)
    slope[...] = sigma * (1.0 + pre * (1.0 - sigma))
    feature = (v + pre * sigma).reshape(4, CELLS, CH)
    pooled = jnp.sum(feature, axis=1) / CELLS
    for copy in copies[4:]:
        copy.wait()
    at = (row_iota((4, 128)), col_iota((4, 128)))
    extra = jnp.zeros((4, 128), f32)
    for slot in range(4):
        alive = jnp.logical_and(slot < counts[0], valid[slot] == 1)
        here = at[0] == slot
        extra = jnp.where(
            jnp.logical_and(here, at[1] == 0), jnp.where(alive, 1.0, 0.0).astype(f32), extra
        )
        extra = jnp.where(
            jnp.logical_and(here, at[1] == 1), pairs[slot].astype(f32), extra
        )
    packed = jnp.concatenate(
        [pooled[:, :256], jnp.concatenate([pooled[:, 256:], extra], axis=1)], axis=0
    )
    pair = jnp.concatenate([packed, packed], axis=0).astype(bf16)
    for at_row in range(0, 256, 16):
        message[at_row : at_row + 16, :] = pair


def scores_of(unit_b, others, ids, lanes):
    return jnp.where(ids == lanes, 0.0, jnp.exp(mm(unit_b, others, NT) / tau_value))


def normalized(pooled, head):
    proj = mm(pooled, head)
    inv = lax.rsqrt(jnp.sum(proj * proj, axis=1, keepdims=True) + norm_eps)
    return proj * inv, inv


def projected_grad(mixing, unit_b, unit, inv):
    dunit = mm(mixing, unit_b) * (loss_scale / tau_value)
    along = jnp.sum(unit * dunit, axis=1, keepdims=True)
    return ((dunit - unit * along) * inv).astype(bf16)


def slot_rows(gathered, home):
    lane = col_iota((home.shape[0], 256))
    first = mm(jnp.where(lane == home, 1.0, 0.0).astype(bf16), gathered)
    second = mm(jnp.where(lane == home + 4, 1.0, 0.0).astype(bf16), gathered)
    pooled = jnp.concatenate([first, second[:, :128]], axis=1).astype(bf16)
    return pooled, second[:, 128:129], second[:, 129:130]


def contrast(gathered, head, rank):
    slot = row_iota((128, 1))
    pooled, live, pairs = slot_rows(gathered, ((slot >> 2) << 3) + (slot & 3))
    own_slot = row_iota((16, 1))
    own_pooled, own_live, own_pairs = slot_rows(
        gathered, jnp.where(own_slot < 4, 8 * rank + own_slot, -8)
    )
    unit, inv = normalized(pooled, head)
    own_unit, own_inv = normalized(own_pooled, head)
    unit_b = unit.astype(bf16)
    j = col_iota((128, 128))
    same = slot == j

    def across(column):
        return jnp.sum(jnp.where(same, column, 0.0), axis=0, keepdims=True)

    live_row = across(live)

    def weights(expo, live, pairs):
        mate = pairs == col_iota(expo.shape).astype(f32)
        total = jnp.sum(expo * live_row, axis=1, keepdims=True)
        share = live * jnp.sum(jnp.where(mate, live_row, 0.0), axis=1, keepdims=True)
        coef = (share / total).astype(bf16).astype(f32)
        return coef, 2.0 * jnp.where(mate, share, 0.0)

    expo = scores_of(unit_b, unit_b, slot, j)
    own_expo = scores_of(own_unit.astype(bf16), unit_b, own_slot + 4 * rank, col_iota((16, 128)))
    coef, drawn = weights(expo, live, pairs)
    own_coef, own_drawn = weights(own_expo, own_live, own_pairs)
    coef_row = across(coef)
    mixing = expo * (coef * live_row + coef_row * live) - drawn
    own_mixing = own_expo * (own_coef * live_row + coef_row * own_live) - own_drawn
    dproj = projected_grad(own_mixing.astype(bf16), unit_b, own_unit, own_inv)
    dpooled = mm(dproj, head, NT).astype(bf16)
    mine = jnp.where(
        col_iota((16, CH)) == row_iota((16, CH)) + 12 * rank, 1.0, 0.0
    ).astype(bf16)
    pooled_mine = mm(mine, pooled, NT).astype(bf16)
    return dpooled[:4].astype(f32), (mixing.astype(bf16), unit, inv, pooled_mine)


def split_kernel(saved, order, mixing, unit, inv, mine, head_out, *outs):
    _, _, y, x, c = position()
    m = row_iota((CH, 1))
    q = (m * 43691) >> 19
    i = m - 12 * q
    j, k = q & 3, q >> 3
    core = c ^ ((q >> 2) & 1)
    flip_x = jnp.where((j == 3) | ((j > 0) & (core == 0)), 3, 0)
    flip_y = jnp.where((j == 3) | ((j > 0) & (core == 1)), 3, 0)
    to_y = y ^ (k >> 1) ^ flip_y
    to_x = x ^ (k & 1) ^ flip_x
    to_core = core ^ jnp.where(j == 2, 1, 0)
    channel = to_y * 96 + to_x * 24 + to_core * 12 + i
    pick = jnp.where(col_iota((CH, CH)) == channel, 1.0, 0.0).astype(bf16)
    turned = mm(pick, saved[...], NT).astype(bf16)
    for k, out in enumerate(outs):
        out[...] = turned[96 * k : 96 * k + 96]

    @pl.when(lax.axis_index("section") == 3)
    def _():
        units = unit[...]
        dproj = projected_grad(mixing[...], units.astype(bf16), units, inv[:, :1])
        head_out[...] = mm(mine[...], dproj)


def top_kernel(
    gathered, head, slope, w, message, dpre_out, mixing_out, unit_out, inv_out, mine_out
):
    section, rank, _, _, _ = position()

    @pl.when(section == 3)
    def _():
        dpooled, (mixing, unit, inv, mine) = contrast(gathered[...], head[...], rank)
        mixing_out[...] = mixing
        unit_out[...] = unit
        inv_out[...] = jnp.broadcast_to(inv, (128, 128))
        mine_out[...] = mine
        top = (dpooled / CELLS).astype(bf16).astype(f32)
        cot = jnp.broadcast_to(top[:, None, :], (4, CELLS, CH)).reshape(ROWS, CH)
        dpre = (cot * slope[...]).astype(bf16)
        dpre_out[...] = dpre
        below = cot + conv_back(dpre.astype(f32), w)
        message[...] = below.astype(bf16)


def relay(active, arrived, slope, w, message, dpre_out):
    @pl.when(lax.axis_index("section") == active)
    def _():
        cot = arrived[...].astype(f32)
        dpre = (cot * slope[...]).astype(bf16)
        dpre_out[...] = dpre
        below = cot + conv_back(dpre.astype(f32), w)
        message[...] = below.astype(bf16)


def relay2_kernel(arrived, slope, w, head_grad, message, dpre_out):
    relay(2, arrived, slope, w, message, dpre_out)

    @pl.when(lax.axis_index("section") == 3)
    def _():
        message[:16, :] = head_grad[:, :384].astype(bf16)


def relay1_kernel(arrived, slope, w, head_grad, message, dpre_out):
    relay(1, arrived, slope, w, message, dpre_out)
    section = lax.axis_index("section")

    @pl.when(section == 3)
    def _():
        message[:16, :] = head_grad[:, :384].astype(bf16)

    @pl.when(section == 0)
    def _():
        message[:16, :] = arrived[:16, :]


def bottom_kernel(arrived, slope, dpre3, dpre2, dpre1, *refs):
    section = lax.axis_index("section")
    dpre_out = refs[-1]
    for at, held in ((3, dpre3), (2, dpre2), (1, dpre1)):

        @pl.when(section == at)
        def _():
            dpre_out[...] = held[...]

    @pl.when(section == 0)
    def _():
        dpre_out[...] = (arrived[...].astype(f32) * slope[...]).astype(bf16)


def last_kernel(arrived, earlier, dpre, w, head_grad, msg3, msg2, msg1, own, grads, head_out):
    section = lax.axis_index("section")

    @pl.when(section == 3)
    def _():
        grads[...] = msg3[...]
        head_out[...] = head_grad[:12, 384:]

    for at, sent in ((2, msg2), (1, msg1)):

        @pl.when(section == at)
        def _():
            grads[...] = sent[...]
            head_out[...] = arrived[:16, at * 128 : at * 128 + 128].astype(f32)[:12]

    @pl.when(section == 0)
    def _():
        below = arrived[...].astype(f32) + conv_back(dpre[...].astype(f32), w)
        grads[...] = below.astype(bf16)
        head_out[...] = earlier[:16, :128].astype(f32)[:12]


def stack_kernel(*refs):
    near, far, out, scratch = refs[:4], refs[4:8], refs[9], refs[10]
    r = col_iota((48, 128))
    ph, pw = (r >> 3) & 3, r & 7
    for g in range(8):
        held = near[g][0:48, :] if g < 4 else far[g - 4][48:96, :]
        v = held.astype(f32)
        for tap in range(9):
            dh, dw = tap // 3 - 1, tap % 3 - 1
            shift = (-(8 * dh + dw)) % 128
            moved = pltpu.roll(v, shift, 1) if shift else v
            inside = (ph + dh >= 0) & (ph + dh < 4) & (pw + dw >= 0) & (pw + dw < 8)
            moved = jnp.where(inside, moved, 0.0)
            scratch[48 * tap : 48 * tap + 48, 128 * g : 128 * g + 128] = moved.astype(bf16)
    m = row_iota((448, 1))
    j = (m * 37450) >> 22
    rest = m - 112 * j
    i = (rest * 7282) >> 16
    source = jnp.where(rest < 108, (rest - 9 * i) * 48 + j * 12 + i, -1)
    pick = jnp.where(col_iota((448, 432)) == source, 1.0, 0.0).astype(bf16)
    out[...] = mm(pick, scratch[...]).astype(bf16)


def wgrad_kernel(stack, *refs):
    grads, outs = refs[:8], refs[8:]
    rows = jnp.concatenate([g[...] for g in grads], axis=0)
    total = mm(stack[...], rows)
    outs[0][...] = total[:112]
    outs[1][...] = total[112:336].astype(bf16)
    outs[2][...] = total[336:].astype(bf16)


def sum_kernel(own, pair, crossed, diagonal, out):
    total = own[...] + pair[:112, :].astype(f32)
    total = total + crossed[112:, :].astype(f32)
    total = total + diagonal[...].astype(f32)
    out[...] = total[:108].reshape(108, 1, CH)


def call(kernel, ins, outs, scratch=(), aliases=None):
    run = pl.pallas_call(
        kernel,
        out_shape=outs,
        in_specs=[pl.BlockSpec(memory_space=space) for space in ins],
        out_specs=jax.tree.map(
            lambda _: pl.BlockSpec(memory_space=VMEM), outs, is_leaf=lambda o: not isinstance(o, tuple)
        ),
        scratch_shapes=list(scratch),
        input_output_aliases=aliases or {},
        compiler_params=pltpu.CompilerParams(vmem_limit_bytes=24 << 20),
    )

    def with_operands(*operands):
        return run(
            *[
                value
                if space is SMEM
                else pltpu.with_memory_space_constraint(value, space)
                for value, space in zip(operands, ins, strict=True)
            ]
        )

    return with_operands


def sds(shape, dtype):
    return jax.ShapeDtypeStruct(shape, dtype)


def per_device(saved, kernels, head, counts, pairs, valid):
    ranks = lax.axis_size("dp")
    act = VMEM((ROWS, CH), bf16)
    piece = VMEM((96, 128), bf16)
    gather = (0, 2, 8, 10)

    def swap(value, bits, odd_bits=None):
        pairs_of = [(d, d ^ (odd_bits if odd_bits and d & 1 else bits)) for d in range(ranks)]
        return lax.ppermute(value, "dp", pairs_of)

    def relayed(value, pairs_of):
        both = [(a, b) for a, b in pairs_of] + [(b, a) for a, b in pairs_of]
        return lax.ppermute(value, "section", both)

    slope, announce, rows, w, head = call(
        forward_kernel,
        [HBM] * 3 + [SMEM] + [HBM] * 2,
        (
            VMEM((ROWS, CH), f32),
            VMEM((256, 256), bf16),
            act,
            VMEM((3, 3, CH, CH), bf16),
            VMEM((CH, EMB), bf16),
        ),
        [SMEM((4,), jnp.int32), SMEM((4,), jnp.int32), pltpu.SemaphoreType.DMA((7,))],
    )(
        saved.reshape(ROWS, CH),
        jnp.transpose(kernels[0], (1, 2, 0, 3)),
        head,
        counts,
        pairs,
        valid,
    )
    gathered = lax.all_to_all(announce.reshape(32, 8, 256), "dp", 0, 0, tiled=True)
    msg3, dpre3, *for_head = call(
        top_kernel,
        [VMEM] * 4,
        (act, act, VMEM((128, 128), bf16), VMEM((128, EMB), f32), VMEM((128, 128), f32))
        + (VMEM((16, 128), bf16),),
    )(gathered.reshape(256, 256), head, slope, w)
    arrived = relayed(msg3, [(3, 2), (1, 0)])
    head_grad, *split = call(
        split_kernel, [VMEM] * 6, (VMEM((16, EMB), f32),) + (piece,) * 4
    )(rows, msg3, *for_head)
    near = [split[0]] + [swap(split[k], gather[k]) for k in range(1, 4)]
    msg2, dpre2 = call(relay2_kernel, [VMEM] * 4, (act, act))(arrived, slope, w, head_grad)
    arrived = earlier = relayed(msg2, [(2, 1), (3, 0)])
    msg1, dpre1 = call(relay1_kernel, [VMEM] * 4, (act, act))(arrived, slope, w, head_grad)
    arrived = relayed(msg1, [(1, 0), (3, 2)])
    far = [swap(value, 1) for value in near]
    dpre = call(bottom_kernel, [VMEM] * 9, act)(
        arrived, slope, dpre3, dpre2, dpre1, *far
    )
    near_grads = [dpre] + [swap(dpre, gather[k]) for k in range(1, 4)]
    stack = call(
        stack_kernel, [VMEM] * 9, VMEM((448, 1024), bf16), [VMEM((432, 1024), bf16)]
    )(*near, *far, dpre)
    far_grads = [swap(value, 1) for value in near_grads]
    own, pair, diagonal = call(
        wgrad_kernel,
        [VMEM] * 9,
        (VMEM((112, CH), f32), VMEM((224, CH), bf16), VMEM((112, CH), bf16)),
    )(stack, *near_grads, *far_grads)
    pair = swap(pair, 6, 24)
    diagonal = swap(diagonal, 30)
    crossed = swap(pair, 1)
    grads, head_grad = call(
        last_kernel, [VMEM] * 9, (sds((ROWS, CH), bf16), sds((12, 128), f32))
    )(arrived, earlier, dpre, w, head_grad, msg3, msg2, msg1, own)
    wgrad = call(sum_kernel, [VMEM] * 4, sds((108, 1, CH), f32))(own, pair, crossed, diagonal)
    return (
        grads.reshape(saved.shape),
        wgrad.reshape(1, 12, 3, 3, CH),
        head_grad,
    )


def solution(mesh):
    return jax.shard_map(
        per_device,
        mesh=mesh,
        in_specs=(
            P("section", "dp", None, None, None),
            P("section", None, None, None, None),
            P(),
            P("dp"),
            P("dp"),
            P("dp"),
        ),
        out_specs=(
            P("section", "dp", None, None, None),
            P("section", "dp", None, None, None),
            P("dp", "section"),
        ),
        check_vma=False,
    )
```
